512 devices in a mesh: node: 64 (over y, x, core), board: 8 (over z).
Axes of the slice: x: 4, y: 8, z: 8, core: 2. Of those that a mesh axis runs over, the one named last changes fastest.
Arguments:
- logits: float32 [8, 4, 2048, 1326], P('board', None, 'node'), may hold values from -310 to 310
- pot_size: float32 [4, 2048], P(None, 'node'), may hold values from 1 to 20
- node_type: int32 [4, 2048], P(None, 'node'), may hold values from 0 to 2, as said below
- parent_slot: int32 [4, 2048], P(None, 'node'), may hold values from 0 to 2047, as said below
- range_one: float32 [8, 1326], P('board'), may hold values from 0.05 to 1
- range_two: float32 [8, 1326], P('board'), may hold values from 0.05 to 1
- hand_rank: int32 [8, 1326], P('board'), may hold values from 0 to 7461
- live_mask: int32 [8, 1326], P('board'), may hold values 0 or 1
Outputs:
- new_logits: float32 [8, 4, 2048, 1326], P('board', None, 'node')
- values_half: float32 [8, 4, 2048, 1326], P('board', None, 'node')
The draws below stay inside these ranges and needn't reach their ends.
Inputs may be any that keep to these rules, and one draw needn't show every extreme that they name: `node_type`: 0 marks an inner node. At each level but the last, each aligned group of four slots holds exactly one node of type 0; the last level holds none. `parent_slot`: at level 0 every entry is 0. At a level above 0 the four nodes of an aligned group of four share one parent, a node of type 0 at the level before, and every such node is the parent of exactly one group; the parent's group index is the group's own index minus an offset of 0 to 7, one offset a level, modulo 2048 / 4.
All inputs are finite; a program needn't handle non-finite values. No bound on the sum of `live_mask` on one device may be relied on, other than what follows from the above.
Results may differ from the reference program's by a relative error of at most 0.0003.
Values sent between devices are 32-bit elements; how exact they have to be, the bound alone decides.
A program may use at most 64 MiB of HBM per device.

```python
import math
import jax
import jax.numpy as jnp
import numpy as np

HANDS = 1326
RANKS = 7462
LEVELS = 4
STEPS = 1
SLOT_DEV = 32
SLOTS = 2048
BOARDS = 8


def draw_logits(key, part):
    full_shape = (BOARDS, LEVELS, SLOTS, HANDS)
    return 1.5 * jax.random.normal(key, full_shape, jnp.float32)


def tree_tables(key):
    groups = SLOTS // 4
    key_off, key_pick, key_kind = jax.random.split(jax.random.fold_in(key, 7), 3)
    offset = jax.random.randint(key_off, (LEVELS,), 0, SLOT_DEV // 4)
    branch = jax.random.randint(key_pick, (LEVELS, groups), 0, 4)
    end_kind = jax.random.randint(key_kind, (LEVELS, SLOTS), 1, 3)
    slot_ids = jnp.arange(SLOTS)
    group_ids = slot_ids // 4
    level_ids = jnp.arange(LEVELS)[:, None]
    owner_group = (group_ids[None, :] - offset[:, None]) % groups
    prev_branch = jnp.concatenate([branch[:1], branch[:-1]], axis=0)
    above_slot = 4 * owner_group + jnp.take_along_axis(prev_branch, owner_group, axis=1)
    parent_table = jnp.where(level_ids == 0, 0, above_slot)
    inner_mask = (slot_ids[None, :] % 4 == branch[:, group_ids]) & (level_ids < LEVELS - 1)
    type_table = jnp.where(inner_mask, 0, end_kind)
    return (parent_table.astype(jnp.int32), type_table.astype(jnp.int32))


def draw_node_type(key, part):
    return tree_tables(key)[1]


def draw_parent_slot(key, part):
    return tree_tables(key)[0]


def touch_ends(drawn, own_key, smallest, top_value):
    shape = drawn.shape
    place = [jax.random.randint(jax.random.fold_in(own_key, axis), (), 0, shape[axis]) for axis in range(len(shape))]
    drawn = drawn.at[tuple(place)].set(smallest)
    longest = shape.index(max(shape))
    place[longest] = (place[longest] + 1) % shape[longest]
    return drawn.at[tuple(place)].set(top_value)


def level_of(key, dims, pieces, low, top_value):
    level = 1.0
    for dim, parts in pieces:
        draws = jax.random.uniform(jax.random.fold_in(jax.random.fold_in(key, 6), dim), (parts,), jnp.float32, low / len(pieces), top_value / len(pieces))
        level = level * jnp.repeat(jnp.exp(draws), dims[dim] // parts).reshape((-1,) + (1,) * (len(dims) - 1 - dim))
    return level


def setup_inputs(seed: int = 0) -> dict:
    keys = jax.random.split(jax.random.key(seed), 9)
    logits = draw_logits(jax.random.fold_in(keys[8], 71), 0)
    pot_size = jnp.clip(jnp.exp(math.log(20.0) - 2.9957323 * jax.random.uniform(keys[1], (LEVELS, SLOTS), jnp.float32) ** level_of(keys[1], (LEVELS, SLOTS), ((1, 64),), -0.2, 0.2)), 1.0, 20.0)
    node_type = draw_node_type(jax.random.fold_in(keys[8], 71), 0)
    parent_slot = draw_parent_slot(jax.random.fold_in(keys[8], 71), 0)
    range_one = jnp.clip(0.05 + 0.95 * jax.random.uniform(keys[4], (BOARDS, HANDS), jnp.float32) ** level_of(keys[4], (BOARDS, HANDS), ((0, 8),), -0.2, 0.2), 0.05, 1.0)
    range_two = jnp.clip(0.05 + 0.95 * jax.random.uniform(keys[5], (BOARDS, HANDS), jnp.float32) ** level_of(keys[5], (BOARDS, HANDS), ((0, 8),), -0.2, 0.2), 0.05, 1.0)
    hand_rank = touch_ends(jax.random.randint(keys[6], (BOARDS, HANDS), 0, RANKS), jax.random.fold_in(keys[6], 1), 0, RANKS - 1).astype(jnp.int32)
    live_mask = touch_ends((jax.random.randint(keys[7], (BOARDS, HANDS), 0, 5) < 4).astype(jnp.int32), jax.random.fold_in(keys[7], 1), 0, 1)
    return dict(logits=logits, pot_size=pot_size, node_type=node_type, parent_slot=parent_slot, range_one=range_one, range_two=range_two, hand_rank=hand_rank, live_mask=live_mask)


step_scale = 0.5
eps_value = 1e-06

def card_pairs(hand_count):
    low_list = []
    high_list = []
    for low_card in range(52):
        for high_card in range(low_card + 1, 52):
            low_list.append(low_card)
            high_list.append(high_card)
    return (np.array(low_list[:hand_count], np.int32), np.array(high_list[:hand_count], np.int32))

def payoff_blocks(hand_rank, live_mask):
    low_np, high_np = card_pairs(hand_rank.shape[-1])
    low_card = jnp.asarray(low_np)
    high_card = jnp.asarray(high_np)
    clash_mask = (low_card[:, None] == low_card[None, :]) | (low_card[:, None] == high_card[None, :]) | (high_card[:, None] == low_card[None, :]) | (high_card[:, None] == high_card[None, :])
    alive_flag = live_mask > 0
    keep_pair = jnp.logical_not(clash_mask)[None] & alive_flag[:, :, None] & alive_flag[:, None, :]
    higher = hand_rank[:, :, None] > hand_rank[:, None, :]
    lower = hand_rank[:, :, None] < hand_rank[:, None, :]
    order_value = jnp.where(higher, 1.0, jnp.where(lower, -1.0, 0.0))
    show_block = jnp.where(keep_pair, order_value, 0.0).astype(jnp.bfloat16)
    compat_block = jnp.where(keep_pair, 1.0, 0.0).astype(jnp.bfloat16)
    return (show_block, compat_block)

def policy(logits):
    full_shape = logits.shape
    grouped = logits.reshape(full_shape[0], full_shape[1], full_shape[2] // 4, 4, full_shape[3])
    return jax.nn.softmax(grouped, axis=3).reshape(full_shape)

def reach_all(strategy, parent_slot, range_one, range_two):
    reach_one = range_one[:, None, :] * strategy[:, 0]
    reach_two = jnp.broadcast_to(range_two[:, None, :], reach_one.shape)
    list_one = [reach_one]
    list_two = [reach_two]
    for depth_idx in range(1, LEVELS):
        above_one = jnp.take(reach_one, parent_slot[depth_idx], axis=1)
        above_two = jnp.take(reach_two, parent_slot[depth_idx], axis=1)
        if depth_idx % 2 == 0:
            reach_one = above_one * strategy[:, depth_idx]
            reach_two = above_two
        else:
            reach_one = above_one
            reach_two = above_two * strategy[:, depth_idx]
        list_one.append(reach_one)
        list_two.append(reach_two)
    return (jnp.stack(list_one, axis=1), jnp.stack(list_two, axis=1))

def terminal_pay(reach_one, reach_two, pot_size, node_type, show_block, compat_block):
    boards = reach_one.shape[0]
    column_count = LEVELS * SLOTS
    level_sign = jnp.where(jnp.arange(LEVELS) % 2 == 0, -1.0, 1.0).astype(jnp.float32)
    show_scale = jnp.where(node_type == 2, pot_size, 0.0).astype(jnp.float32)
    fold_scale = jnp.where(node_type == 1, pot_size, 0.0).astype(jnp.float32) * level_sign[:, None]

    def columns(reach_value, scale_value):
        return (reach_value * scale_value[None, :, :, None]).astype(jnp.bfloat16).reshape(boards, column_count, HANDS)
    show_cols = jnp.concatenate([columns(reach_two, show_scale), columns(reach_one, show_scale)], axis=1)
    fold_cols = jnp.concatenate([columns(reach_two, fold_scale), -columns(reach_one, fold_scale)], axis=1)
    product = jnp.einsum('bij,bnj->bni', show_block.astype(jnp.float32), show_cols.astype(jnp.float32)) + jnp.einsum('bij,bnj->bni', compat_block.astype(jnp.float32), fold_cols.astype(jnp.float32))
    pay_one = product[:, :column_count].reshape(boards, LEVELS, SLOTS, HANDS)
    pay_two = product[:, column_count:].reshape(boards, LEVELS, SLOTS, HANDS)
    return (pay_one, pay_two)

def values_all(strategy, parent_slot, pay_one, pay_two):
    value_one = pay_one[:, LEVELS - 1]
    value_two = pay_two[:, LEVELS - 1]
    found_list = [None] * LEVELS
    found_list[LEVELS - 1] = value_one if (LEVELS - 1) % 2 == 0 else value_two

    def sum_up(term_value, child_level):
        moved = jnp.swapaxes(term_value, 0, 1)
        summed = jax.ops.segment_sum(moved, parent_slot[child_level], num_segments=SLOTS)
        return jnp.swapaxes(summed, 0, 1)
    for depth_idx in range(LEVELS - 2, -1, -1):
        child_level = depth_idx + 1
        weight = strategy[:, child_level]
        if child_level % 2 == 0:
            term_one = weight * value_one
            term_two = value_two
        else:
            term_one = value_one
            term_two = weight * value_two
        value_one = pay_one[:, depth_idx] + sum_up(term_one, child_level)
        value_two = pay_two[:, depth_idx] + sum_up(term_two, child_level)
        found_list[depth_idx] = value_one if depth_idx % 2 == 0 else value_two
    return jnp.stack(found_list, axis=1)

def operate(point, pot_size, node_type, parent_slot, range_one, range_two, show_block, compat_block):
    strategy = policy(point)
    reach_one, reach_two = reach_all(strategy, parent_slot, range_one, range_two)
    pay_one, pay_two = terminal_pay(reach_one, reach_two, pot_size, node_type, show_block, compat_block)
    return values_all(strategy, parent_slot, pay_one, pay_two)

def rate_for(values_found):
    square_sum = jnp.sum(values_found * values_found)
    return step_scale / jnp.sqrt(square_sum / values_found.size + eps_value)

def reference(logits, pot_size, node_type, parent_slot, range_one, range_two, hand_rank, live_mask):
    show_block, compat_block = payoff_blocks(hand_rank, live_mask)
    current = logits
    values_half = logits
    for turn_idx in range(STEPS):
        anchor_mix = 1.0 / (turn_idx + 2)
        base_point = current + anchor_mix * (logits - current)
        values_now = operate(current, pot_size, node_type, parent_slot, range_one, range_two, show_block, compat_block)
        half_point = base_point + rate_for(values_now) * values_now
        values_half = operate(half_point, pot_size, node_type, parent_slot, range_one, range_two, show_block, compat_block)
        current = base_point + rate_for(values_half) * values_half
    return (current, values_half)
```

```python
import functools

import jax
import jax.numpy as jnp
import numpy as np
from jax import lax
from jax.experimental import pallas as pl
from jax.experimental.pallas import tpu as pltpu
from jax.sharding import PartitionSpec as P

HANDS = 1326
PAD = 1408
CHUNKS = PAD // 128
LEVELS = 4
SLOT_DEV = 32
GROUPS = SLOT_DEV // 4
NODES = 64
BOARDS = 8
ALL_GROUPS = NODES * GROUPS
ENTRIES = BOARDS * LEVELS * NODES * SLOT_DEV * HANDS
STEP_SCALE = 0.5
EPS = 1e-06
ROWS = 48 * 3
ROWS_ALL = ROWS + 32
F32 = jnp.float32
BF16 = jnp.bfloat16
MESH = pl.DeviceIdType.MESH


def card_rows():
    table = np.zeros((64, PAD), np.float32)
    hand = 0
    for low in range(52):
        for high in range(low + 1, 52):
            if hand < HANDS:
                table[low, hand] = 1.0
                table[high, hand] = 1.0
                hand += 1
    return table


def iota(shape, dim):
    return lax.broadcasted_iota(jnp.int32, shape, dim)


def pick_rows(onehot, rows):
    high = rows.astype(BF16)
    rest = rows - high.astype(F32)
    mid = rest.astype(BF16)
    low = (rest - mid.astype(F32)).astype(BF16)
    parts = jnp.concatenate([high, mid, low], axis=0)
    pick = jnp.where(onehot, 1.0, 0.0)
    pick = jnp.concatenate([pick, pick, pick], axis=1).astype(BF16)
    return jnp.dot(pick, parts, preferred_element_type=F32)


def kernel(
    logits,
    pot,
    kind,
    parent,
    range_one,
    range_two,
    rank,
    live,
    cards,
    out_logits,
    out_values,
    own,
    own_pot,
    own_kind,
    parent_s,
    rng1,
    rng2,
    rank_v,
    live_v,
    cards_v,
    win0,
    win2,
    win3a,
    win3b,
    pot0,
    pot2,
    pot3,
    kind0,
    kind2,
    kind3,
    reach1,
    reach2,
    rank_p,
    dead_p,
    lhs_cards,
    rhs_cards,
    table,
    zbuf,
    strat,
    qbuf,
    cols,
    blocks,
    pay,
    part_a,
    part_b,
    ring_a1,
    ring_b1,
    ring_a2,
    ring_b2,
    ret0,
    ret2,
    ret3a,
    ret3b,
    fin_values,
    fin_logits,
    in_sem,
    out_sem,
    halo_send,
    halo_recv,
    ret_send,
    ret_recv,
    ar_send_a,
    ar_send_b,
    ar_recv_a1,
    ar_recv_b1,
    ar_recv_a2,
    ar_recv_b2,
):
    node = lax.axis_index("node")
    board = lax.axis_index("board")
    core = lax.rem(node, 2)
    chip = node // 2

    def at_node(step):
        return {"node": lax.rem(node + step + NODES, NODES), "board": board}

    def peer_a(j):
        spot = lax.rem(board * 2 + core + j, 16)
        return {"node": chip * 2 + lax.rem(spot, 2), "board": spot // 2}

    def peer_b(j):
        return {"node": lax.rem(chip + j, 32) * 2 + core, "board": board}

    barrier = pltpu.get_barrier_semaphore()
    for step in (1, -1, 2, -2):
        pl.semaphore_signal(barrier, inc=1, device_id=at_node(step), device_id_type=MESH)

    @pl.loop(1, 16)
    def _(j):
        pl.semaphore_signal(barrier, inc=1, device_id=peer_a(j), device_id_type=MESH)

    @pl.loop(1, 32)
    def _(j):
        pl.semaphore_signal(barrier, inc=1, device_id=peer_b(j), device_id_type=MESH)

    loads = [
        pltpu.make_async_copy(src, dst, in_sem.at[idx])
        for idx, (src, dst) in enumerate(
            [
                (live, live_v),
                (rank, rank_v),
                (cards, cards_v),
                (pot, own_pot),
                (kind, own_kind),
                (parent, parent_s),
                (range_one, rng1),
                (range_two, rng2),
                (logits.at[0], own),
            ]
        )
    ]
    for load in loads:
        load.start()
    for load in loads:
        load.wait()

    def halo(idx, src, dst, step):
        return pltpu.make_async_remote_copy(
            src_ref=src,
            dst_ref=dst,
            send_sem=halo_send.at[idx],
            recv_sem=halo_recv.at[idx],
            device_id=at_node(step),
            device_id_type=MESH,
        )

    halos = [
        halo(0, pot, pot0, 1),
        halo(1, kind, kind0, 1),
        halo(2, pot, pot2, -1),
        halo(3, kind, kind2, -1),
        halo(4, pot, pot3, -2),
        halo(5, kind, kind3, -2),
        halo(6, logits.at[0, 0], win0, 1),
        halo(7, logits.at[0, 2], win2, -1),
        halo(8, logits.at[0, 3], win3a, -1),
        halo(9, logits.at[0, 3, pl.ds(0, 24)], win3b, -2),
    ]
    pl.semaphore_wait(barrier, 4 + 15 + 31)
    for copy in halos:
        copy.start()

    zero_row = jnp.zeros((1, PAD), F32)
    reach1[...] = zero_row
    reach2[...] = zero_row
    rank_p[...] = zero_row
    alive = jnp.where(live_v[...] > 0, 1.0, 0.0)
    reach1[:, 0:HANDS] = rng1[...] * alive
    reach2[:, 0:HANDS] = rng2[...] * alive
    rank_p[:, 0:HANDS] = rank_v[...].astype(F32)
    dead_p[...] = jnp.ones((1, PAD), F32)
    dead_p[:, 0:HANDS] = 1.0 - alive
    dead = dead_p[...]
    lhs_cards[0:48] = cards_v[0:48].astype(BF16)
    rhs_cards[0:48] = cards_v[0:48].astype(BF16)
    tail = cards_v[48:64]
    row = iota((16, PAD), 0)
    lhs_cards[48:64] = jnp.where(row == 4, 1.0, jnp.where(row == 5, dead, tail)).astype(BF16)
    rhs_cards[48:64] = jnp.where(row == 4, dead, jnp.where(row == 5, 1.0, tail)).astype(BF16)

    @pl.loop(0, CHUNKS)
    def _(jb):
        base = pl.multiple_of(jb * 128, 128)
        shared = lax.dot_general(
            lhs_cards[:, pl.ds(base, 128)],
            rhs_cards[...],
            (((0,), (0,)), ((), ())),
            preferred_element_type=F32,
        )
        rank_j = jnp.broadcast_to(rank_p[:, pl.ds(base, 128)], (128, 128)).T
        for ic in range(CHUNKS):
            span = slice(ic * 128, ic * 128 + 128)
            keep = shared[:, span] < 0.5
            order = jnp.clip(rank_p[:, span] - rank_j, -1.0, 1.0)
            blocks[pl.ds(base, 128), span] = jnp.where(keep, order, 0.0).astype(BF16)
            blocks[pl.ds(PAD + base, 128), span] = jnp.where(keep, 1.0, 0.0).astype(BF16)

    def offset(level):
        return jnp.bitwise_and(node * GROUPS - parent_s[level, 0] // 4 + ALL_GROUPS, ALL_GROUPS - 1)

    off1 = offset(1)
    off2 = offset(2)
    off23 = off2 + offset(3)

    for copy in halos[:6]:
        copy.wait()

    lane = iota((8, SLOT_DEV), 1)
    group = iota((8, SLOT_DEV), 0)

    def fill_table(level, shift, windows):
        for k in range(4):
            target = 4 * (group + shift) + k
            pots = jnp.zeros((8, SLOT_DEV), F32)
            kinds = jnp.zeros((8, SLOT_DEV), F32)
            for base, pot_ref, kind_ref in windows:
                hit = lane + base == target
                pots += jnp.where(hit, pot_ref[level : level + 1], 0.0)
                kinds += jnp.where(hit, kind_ref[level : level + 1].astype(F32), 0.0)
            pots = jnp.broadcast_to(jnp.sum(pots, axis=1, keepdims=True), (8, 128))
            kinds = jnp.broadcast_to(jnp.sum(kinds, axis=1, keepdims=True), (8, 128))
            sign = -1.0 if level % 2 == 0 else 1.0
            table[0, level, k] = jnp.where(kinds > 1.5, pots, 0.0)
            table[1, level, k] = jnp.where(jnp.abs(kinds - 1.0) < 0.5, pots, 0.0) * sign
            table[2, level, k] = jnp.where(kinds < 0.5, 1.0, 0.0)

    fill_table(0, -off1, [(-SLOT_DEV, pot0, kind0), (0, own_pot, own_kind)])
    fill_table(1, 0, [(0, own_pot, own_kind)])
    fill_table(2, off2, [(0, own_pot, own_kind), (SLOT_DEV, pot2, kind2)])
    fill_table(
        3,
        off23,
        [(0, own_pot, own_kind), (SLOT_DEV, pot2, kind2), (2 * SLOT_DEV, pot3, kind3)],
    )

    def gather(level, shift, rows):
        count = rows.shape[0]
        out_row = iota((32, count), 0)
        col = iota((32, count), 1)
        want = 4 * (jnp.bitwise_and(out_row, 7) + shift) + out_row // 8
        zbuf[level, :, PAD - 128 : PAD] = jnp.zeros((32, 128), F32)
        zbuf[level, :, 0:HANDS] = pick_rows(col == want, rows)

    gather(1, 0, own[1])
    halos[6].wait()
    gather(0, 8 - off1, jnp.concatenate([win0[...], own[0]], axis=0))
    halos[7].wait()
    gather(2, off2, jnp.concatenate([own[2], win2[...]], axis=0))
    halos[8].wait()
    halos[9].wait()
    gather(
        3,
        off23,
        jnp.concatenate([own[3], win3a[...], win3b[...], jnp.zeros((8, HANDS), F32)], axis=0),
    )

    def put(first_row, span, fold, even, odd):
        pair = jnp.concatenate([even, odd], axis=0).astype(BF16)
        cols[first_row : first_row + 16, pl.ds(span + (PAD if fold else 0), 128)] = pair

    def rounded(value):
        return value.astype(BF16).astype(F32)

    def put_sum(first_row, span, fold, value):
        high = rounded(value)
        put(first_row, span, fold, high, value - high)

    def columns(rate):
        @pl.loop(0, CHUNKS)
        def _(chunk):
            span = pl.multiple_of(chunk * 128, 128)

            def soft(level):
                z = [zbuf[level, 8 * k : 8 * k + 8, pl.ds(span, 128)] for k in range(4)]
                if rate is not None:
                    z = [
                        z[k] + rate * qbuf[level, 8 * k : 8 * k + 8, pl.ds(span, 128)]
                        for k in range(4)
                    ]
                top = jnp.maximum(jnp.maximum(z[0], z[1]), jnp.maximum(z[2], z[3]))
                e = [jnp.exp(x - top) for x in z]
                inv = 1.0 / ((e[0] + e[1]) + (e[2] + e[3]))
                return [x * inv for x in e]

            def inner(level, values):
                return sum(table[2, level, k] * values[k] for k in range(4))

            def both(level, values, sign):
                show = [values[k] * table[0, level, k] for k in range(4)]
                fold = [values[k] * table[1, level, k] for k in range(4)]
                return show, [-x for x in fold] if sign < 0 else fold

            def put_slots(first_row, pairs):
                for fold, values in enumerate(pairs):
                    put(first_row, span, fold, values[0], values[1])
                    put(first_row + 16, span, fold, values[2], values[3])

            def put_sums(first_row, pairs):
                for fold, values in enumerate(pairs):
                    put_sum(first_row, span, fold, sum(rounded(x) for x in values))

            one = reach1[:, pl.ds(span, 128)]
            two = reach2[:, pl.ds(span, 128)]
            if rate is None:
                put_slots(ROWS, both(0, [two] * 4, 1))
            x1 = one * inner(0, soft(0))
            y1 = [two * s for s in soft(1)]
            y2 = inner(1, y1)
            put_slots(0, both(1, [x1] * 4, -1))
            put_sums(32, both(1, y1, 1))
            s2 = soft(2)
            x2 = [x1 * s for s in s2]
            x3 = inner(2, x2)
            put_slots(48, both(2, [y2] * 4, 1))
            put_sums(80, both(2, x2, -1))
            s3 = soft(3)
            y3 = [y2 * s for s in s3]
            put_slots(96, both(3, [x3] * 4, -1))
            put_sums(128, both(3, y3, 1))
            for k in range(4):
                strat[0, 8 * k : 8 * k + 8, pl.ds(span, 128)] = s2[k]
                strat[1, 8 * k : 8 * k + 8, pl.ds(span, 128)] = s3[k]

    def payoffs(rows):
        for first in range(0, PAD, 256):
            last = min(first + 256, PAD)
            pay[0:rows, first:last] = jnp.dot(
                cols[0:rows, :], blocks[:, first:last], preferred_element_type=F32
            )

    def values_up():
        def step(chunk, total):
            span = pl.multiple_of(chunk * 128, 128)

            def get(first_row):
                return pay[first_row : first_row + 8, pl.ds(span, 128)]

            def slots(first_row):
                return [get(first_row + 8 * k) for k in range(4)]

            def summed(first_row):
                return get(first_row) + get(first_row + 8)

            def weighted(which, values):
                return sum(
                    strat[which, 8 * k : 8 * k + 8, pl.ds(span, 128)] * values[k]
                    for k in range(4)
                )

            def joined(level, values, below):
                return [values[k] + table[2, level, k] * below for k in range(4)]

            q3 = slots(96)
            q2 = joined(2, slots(48), summed(128))
            q1 = joined(1, slots(0), summed(80) + weighted(1, q3))
            q0 = joined(0, slots(ROWS), summed(32) + weighted(0, q2))
            for level, q in enumerate((q0, q1, q2, q3)):
                for k in range(4):
                    qbuf[level, 8 * k : 8 * k + 8, pl.ds(span, 128)] = q[k]
                total = total + ((q[0] * q[0] + q[1] * q[1]) + (q[2] * q[2] + q[3] * q[3]))
            return total

        total = lax.fori_loop(0, CHUNKS, step, jnp.zeros((8, 128), F32))
        return jnp.sum(total, axis=0, keepdims=True)

    def exchange(src, ring, count, send_sem, recv_sem, peer):
        def copy(j):
            return pltpu.make_async_remote_copy(
                src_ref=src,
                dst_ref=ring.at[j],
                send_sem=send_sem.at[j],
                recv_sem=recv_sem.at[j],
                device_id=peer(j),
                device_id_type=MESH,
            )

        @pl.loop(1, count)
        def _(j):
            copy(j).start()

        def finish():
            @pl.loop(1, count)
            def _(j):
                copy(j).wait()

        return finish

    def reduce_start(total, ring_a, recv_a):
        part_a[...] = total
        ring_a[0] = total
        return exchange(part_a, ring_a, 16, ar_send_a, recv_a, peer_a)

    def reduce_second(finish, ring_a, ring_b, recv_b):
        finish()
        total = jnp.sum(ring_a[...], axis=0)
        part_b[...] = total
        ring_b[0] = total
        return exchange(part_b, ring_b, 32, ar_send_b, recv_b, peer_b)

    def reduce_rate(finish, ring_b):
        finish()
        total = jnp.sum(jnp.sum(ring_b[...], axis=0), axis=1, keepdims=True)
        return jnp.broadcast_to(STEP_SCALE / jnp.sqrt(total / ENTRIES + EPS), (8, 128))

    columns(None)
    payoffs(ROWS_ALL)
    first = reduce_start(values_up(), ring_a1, ar_recv_a1)
    rate = reduce_rate(reduce_second(first, ring_a1, ring_b1, ar_recv_b1), ring_b1)
    columns(rate)
    payoffs(ROWS)
    first = reduce_start(values_up(), ring_a2, ar_recv_a2)

    def back(idx, src, dst, step):
        return pltpu.make_async_remote_copy(
            src_ref=src,
            dst_ref=dst,
            send_sem=ret_send.at[idx],
            recv_sem=ret_recv.at[idx],
            device_id=at_node(step),
            device_id_type=MESH,
        )

    backs = [
        back(0, qbuf.at[3], ret3a, 1),
        back(1, qbuf.at[3], ret3b, 2),
        back(2, qbuf.at[2], ret2, 1),
        back(3, qbuf.at[0], ret0, -1),
    ]
    for copy in backs:
        copy.start()
    second = reduce_second(first, ring_a2, ring_b2, ar_recv_b2)

    def scatter(level, shift, rows):
        count = rows.shape[0]
        out_row = iota((32, count), 0)
        col = iota((32, count), 1)
        same_slot = jnp.bitwise_and(out_row, 3) == jnp.bitwise_and(col // 8, 3)
        chain = 8 * (col // 32) + jnp.bitwise_and(col, 7)
        hit = jnp.logical_and(same_slot, chain == out_row // 4 + shift)
        fin_values[level] = pick_rows(hit, rows)[:, 0:HANDS]

    scatter(1, 0, qbuf[1])
    backs[3].wait()
    scatter(0, off1, jnp.concatenate([qbuf[0], ret0[...]], axis=0))
    backs[2].wait()
    scatter(2, 8 - off2, jnp.concatenate([ret2[...], qbuf[2]], axis=0))
    backs[0].wait()
    backs[1].wait()
    scatter(3, 16 - off23, jnp.concatenate([ret3b[...], ret3a[...], qbuf[3]], axis=0))
    write_values = pltpu.make_async_copy(fin_values, out_values.at[0], out_sem.at[0])
    write_values.start()
    rate = reduce_rate(second, ring_b2)
    for level in range(LEVELS):
        fin_logits[level] = own[level] + rate[0:1, 0:1] * fin_values[level]
    write_logits = pltpu.make_async_copy(fin_logits, out_logits.at[0], out_sem.at[1])
    write_logits.start()
    write_values.wait()
    write_logits.wait()


def per_device(
    logits, pot_size, node_type, parent_slot, range_one, range_two, hand_rank, live_mask
):
    small = (LEVELS, SLOT_DEV)
    rows = (SLOT_DEV, HANDS)
    wide = (SLOT_DEV, PAD)
    vmem = pltpu.VMEM
    dma = pltpu.SemaphoreType.DMA
    scratch = [
        vmem((LEVELS,) + rows, F32),
        vmem(small, F32),
        vmem(small, jnp.int32),
        pltpu.SMEM(small, jnp.int32),
        vmem((1, HANDS), F32),
        vmem((1, HANDS), F32),
        vmem((1, HANDS), jnp.int32),
        vmem((1, HANDS), jnp.int32),
        vmem((64, PAD), F32),
        vmem(rows, F32),
        vmem(rows, F32),
        vmem(rows, F32),
        vmem((24, HANDS), F32),
        vmem(small, F32),
        vmem(small, F32),
        vmem(small, F32),
        vmem(small, jnp.int32),
        vmem(small, jnp.int32),
        vmem(small, jnp.int32),
        vmem((1, PAD), F32),
        vmem((1, PAD), F32),
        vmem((1, PAD), F32),
        vmem((1, PAD), F32),
        vmem((64, PAD), BF16),
        vmem((64, PAD), BF16),
        vmem((3, LEVELS, 4, 8, 128), F32),
        vmem((LEVELS,) + wide, F32),
        vmem((2,) + wide, F32),
        vmem((LEVELS,) + wide, F32),
        vmem((ROWS_ALL, 2 * PAD), BF16),
        vmem((2 * PAD, PAD), BF16),
        vmem((ROWS_ALL, PAD), F32),
        vmem((1, 128), F32),
        vmem((1, 128), F32),
        vmem((16, 1, 128), F32),
        vmem((32, 1, 128), F32),
        vmem((16, 1, 128), F32),
        vmem((32, 1, 128), F32),
        vmem(wide, F32),
        vmem(wide, F32),
        vmem(wide, F32),
        vmem(wide, F32),
        vmem((LEVELS,) + rows, F32),
        vmem((LEVELS,) + rows, F32),
        dma((9,)),
        dma((2,)),
        dma((10,)),
        dma((10,)),
        dma((4,)),
        dma((4,)),
        dma((16,)),
        dma((32,)),
        dma((16,)),
        dma((32,)),
        dma((16,)),
        dma((32,)),
    ]
    whole = jax.ShapeDtypeStruct(logits.shape, F32)
    hbm = pl.BlockSpec(memory_space=pl.ANY)
    return pl.pallas_call(
        kernel,
        name="extragradient",
        out_shape=(whole, whole),
        in_specs=[hbm] * 9,
        out_specs=(hbm, hbm),
        scratch_shapes=scratch,
        compiler_params=pltpu.CompilerParams(
            collective_id=0, has_side_effects=True, vmem_limit_bytes=48 * 1024 * 1024
        ),
    )(
        logits,
        pot_size,
        node_type,
        parent_slot,
        range_one,
        range_two,
        hand_rank,
        live_mask,
        jnp.asarray(card_rows()),
    )


def solution(mesh):
    placed = (
        P("board", None, "node", None),
        P(None, "node"),
        P(None, "node"),
        P(None, "node"),
        P("board", None),
        P("board", None),
        P("board", None),
        P("board", None),
    )
    return jax.shard_map(
        per_device,
        mesh=mesh,
        in_specs=placed,
        out_specs=(P("board", None, "node", None), P("board", None, "node", None)),
        check_vma=False,
    )
```

```python
import functools

import jax
import jax.numpy as jnp
import numpy as np
from jax import lax
from jax.experimental import pallas as pl
from jax.experimental.pallas import tpu as pltpu
from jax.sharding import PartitionSpec as P

HANDS = 1326
PAD = 1408
CHUNKS = PAD // 128
LEVELS = 4
SLOT_DEV = 32
GROUPS = SLOT_DEV // 4
NODES = 64
BOARDS = 8
ALL_GROUPS = NODES * GROUPS
ENTRIES = BOARDS * LEVELS * NODES * SLOT_DEV * HANDS
STEP_SCALE = 0.5
EPS = 1e-06
CHIPS = NODES // 2
PEERS_A = 2 * BOARDS
ROW1, ROW2, ROW3, ROWS = 32, 80, 128, 176
F32 = jnp.float32
BF16 = jnp.bfloat16
MESH = pl.DeviceIdType.MESH


KEEP_A = 4
CARDS = 52
DEEP = PAD + 3 * 64


def card_rows():
    table = np.zeros((64, PAD), np.float32)
    hand = 0
    for low in range(52):
        for high in range(low + 1, 52):
            if hand < HANDS:
                table[low, hand] = 1.0
                table[high, hand] = 1.0
                hand += 1
    return table


def iota(shape, dim):
    return lax.broadcasted_iota(jnp.int32, shape, dim)


def three_parts(value):
    high = value.astype(BF16)
    rest = value - high.astype(F32)
    mid = rest.astype(BF16)
    return [high, mid, (rest - mid.astype(F32)).astype(BF16)]


def pick_rows(pick, rows):
    parts = jnp.concatenate(three_parts(rows), axis=0)
    pick = jnp.concatenate([pick, pick, pick], axis=1).astype(BF16)
    return jnp.dot(pick, parts, preferred_element_type=F32)


def third(value):
    return jnp.right_shift(value * 43, 7)


def kernel(
    logits,
    pot,
    kind,
    parent,
    range_one,
    range_two,
    rank,
    live,
    cards,
    cards_t,
    out_logits,
    out_values,
    own,
    own_pot,
    own_kind,
    parent_s,
    rng1,
    rng2,
    rank_v,
    live_v,
    cards_v,
    cards_tv,
    diffs,
    win0a,
    win0b,
    win1,
    win2,
    win3a,
    win3b,
    near_pot,
    near_kind,
    reach1,
    reach2,
    rank_p,
    dead_p,
    rhs_cards,
    table,
    zbuf,
    strat,
    qbuf,
    qsend,
    cols,
    folds,
    blocks,
    pay,
    part_a,
    part_b,
    ring_a1,
    ring_b1,
    ring_a2,
    ring_b2,
    ret0a,
    ret0b,
    ret1,
    ret2,
    ret3a,
    ret3b,
    hold,
    known,
    in_sem,
    halo_send,
    halo_recv,
    ret_send,
    ret_recv,
    ar_send_a,
    ar_send_b,
    ar_recv_a1,
    ar_recv_b1,
    ar_recv_a2,
    ar_recv_b2,
):
    node = lax.axis_index("node")
    board = lax.axis_index("board")
    core = lax.rem(node, 2)
    chip = node // 2

    def at_node(step):
        return {"node": lax.rem(node + step + NODES, NODES), "board": board}

    def at_board(step):
        return {"node": node, "board": lax.rem(board + step + BOARDS, BOARDS)}

    def peer_a(j):
        spot = lax.rem(board * 2 + core + j, PEERS_A)
        return {"node": chip * 2 + lax.rem(spot, 2), "board": spot // 2}

    def peer_b(j):
        return {"node": lax.rem(chip + j, CHIPS) * 2 + core, "board": board}

    loads = [
        pltpu.make_async_copy(src, dst, in_sem.at[idx])
        for idx, (src, dst) in enumerate(
            [
                (live, live_v),
                (rank, rank_v),
                (cards, cards_v),
                (cards_t, cards_tv),
                (pot, own_pot),
                (kind, own_kind),
                (parent, parent_s),
                (range_one, rng1),
                (range_two, rng2),
                (logits.at[0], own),
            ]
        )
    ]

    barrier = pltpu.get_barrier_semaphore()
    close = [at_node(step) for step in (1, -1, 2, -2)]
    if BOARDS > 1:
        close += [at_board(step) for step in (1, -1)]
    for peer in close:
        pl.semaphore_signal(barrier, inc=1, device_id=peer, device_id_type=MESH)
    for load in loads:
        load.start()
    rounds = []
    step = 1
    while step < CHIPS // 2 or step <= BOARDS // 2:
        peers = []
        if step < CHIPS // 2:
            peers += [at_node(2 * step), at_node(-2 * step)]
        if step < BOARDS // 2:
            peers += [at_board(step), at_board(-step)]
        elif step == BOARDS // 2:
            peers += [at_board(step)]
        rounds.append(peers)
        step *= 2

    def announce(idx):
        if idx < len(rounds):
            for peer in rounds[idx]:
                pl.semaphore_signal(known.at[idx], inc=1, device_id=peer, device_id_type=MESH)

    def heard(idx):
        if idx < len(rounds):
            pl.semaphore_wait(known.at[idx], len(rounds[idx]))

    def halo(idx, src, dst, step):
        return pltpu.make_async_remote_copy(
            src_ref=src,
            dst_ref=dst,
            send_sem=halo_send.at[idx],
            recv_sem=halo_recv.at[idx],
            device_id=at_node(step),
            device_id_type=MESH,
        )

    halos = []
    for spot, step in enumerate((1, -1, 2, -2)):
        halos.append(halo(2 * spot, pot, near_pot.at[spot], step))
        halos.append(halo(2 * spot + 1, kind, near_kind.at[spot], step))
    sends = [
        halo(8, diffs.at[1, pl.ds(0, 16)], win1, 1),
        halo(9, diffs.at[0], win0a, 1),
        halo(10, diffs.at[0, pl.ds(0, 16)], win0b, 2),
        halo(11, diffs.at[2, pl.ds(0, 16)], win2, -1),
        halo(12, diffs.at[3], win3a, -1),
        halo(13, diffs.at[3, pl.ds(0, 8)], win3b, -2),
    ]
    pl.semaphore_wait(barrier, len(close))
    for copy in halos:
        copy.start()
    announce(0)
    loads[-1].wait()

    out_row = iota((24, SLOT_DEV), 0)
    col = iota((24, SLOT_DEV), 1)
    for level, copies in ((1, sends[0:1]), (0, sends[1:3]), (2, sends[3:4]), (3, sends[4:6])):
        group = third(out_row)
        slot = out_row - 3 * group + 1
        group = GROUPS - 1 - group if level < 2 else group
        pick = jnp.where(col == 4 * group + slot, 1.0, jnp.where(col == 4 * group, -1.0, 0.0))
        diffs[level, :, 0:HANDS] = pick_rows(pick, own[level])
        diffs[level, :, HANDS:PAD] = jnp.zeros((24, PAD - HANDS), F32)
        for copy in copies:
            copy.start()
    for load in loads[:-1]:
        load.wait()

    zero_row = jnp.zeros((1, PAD), F32)
    reach1[...] = zero_row
    reach2[...] = zero_row
    rank_p[...] = zero_row
    alive = jnp.where(live_v[...] > 0, 1.0, 0.0)
    reach1[:, 0:HANDS] = rng1[...] * alive
    reach2[:, 0:HANDS] = rng2[...] * alive
    rank_p[:, 0:HANDS] = rank_v[...].astype(F32)
    dead_p[...] = jnp.ones((1, PAD), F32)
    dead_p[:, 0:HANDS] = 1.0 - alive
    dead = dead_p[...]
    row = iota((16, PAD), 0)
    head = cards_v[0:48]
    tail = cards_v[48:64]
    rhs_cards[0:48] = head.astype(BF16)
    rhs_cards[48:64] = jnp.where(row == CARDS - 48, dead, tail).astype(BF16)
    lively = 1.0 - dead
    for part in range(3):
        top = PAD + 64 * part
        blocks[top : top + 48] = (-head * lively).astype(BF16)
        blocks[top + 48 : top + 64] = jnp.where(row == CARDS - 48, lively, -tail * lively).astype(BF16)

    @pl.loop(0, CHUNKS)
    def _(jb):
        base = pl.multiple_of(jb * 128, 128)
        rank_j = jnp.broadcast_to(rank_p[:, pl.ds(base, 128)], (128, 128)).T
        mine = cards_tv[pl.ds(base, 128)]
        for first in range(0, PAD, 256):
            last = min(first + 256, PAD)
            shared = jnp.dot(mine, rhs_cards[:, first:last], preferred_element_type=F32)
            for start in range(first, last, 128):
                span = slice(start, start + 128)
                keep = shared[:, start - first : start - first + 128] < 0.5
                order = jnp.clip(rank_p[:, span] - rank_j, -1.0, 1.0)
                blocks[pl.ds(base, 128), span] = jnp.where(keep, order, 0.0).astype(BF16)

    def offset(level):
        return jnp.bitwise_and(node * GROUPS - parent_s[level, 0] // 4 + ALL_GROUPS, ALL_GROUPS - 1)

    off1 = offset(1)
    off2 = offset(2)
    off3 = offset(3)

    def places(chain):
        late = jnp.logical_and(chain >= KEEP_A, chain + off2 >= GROUPS)
        first = jnp.where(late, chain - GROUPS, chain)
        return [first - off1, first, first + off2, first + off2 + off3]

    heard(0)
    announce(1)
    for copy in halos:
        copy.wait()

    lane = iota((8, SLOT_DEV), 1)
    spots = places(iota((8, SLOT_DEV), 0))
    near = {1: 1, -1: 0, 2: 3, -2: 2}

    def fill_table(level, steps):
        for k in range(4):
            pots = jnp.zeros((8, SLOT_DEV), F32)
            kinds = jnp.zeros((8, SLOT_DEV), F32)
            for step in steps:
                pot_row = own_pot[level : level + 1] if step == 0 else near_pot[near[step], level : level + 1]
                kind_row = own_kind[level : level + 1] if step == 0 else near_kind[near[step], level : level + 1]
                hit = lane + SLOT_DEV * step == 4 * spots[level] + k
                pots += jnp.where(hit, pot_row, 0.0)
                kinds += jnp.where(hit, kind_row.astype(F32), 0.0)
            pots = jnp.broadcast_to(jnp.sum(pots, axis=1, keepdims=True), (8, 128))
            kinds = jnp.broadcast_to(jnp.sum(kinds, axis=1, keepdims=True), (8, 128))
            sign = -1.0 if level % 2 == 0 else 1.0
            table[0, level, k] = jnp.where(kinds > 1.5, pots, 0.0)
            table[1, level, k] = jnp.where(jnp.abs(kinds - 1.0) < 0.5, pots, 0.0) * sign
            table[2, level, k] = jnp.where(kinds < 0.5, 1.0, 0.0)

    fill_table(0, (-2, -1, 0))
    fill_table(1, (-1, 0))
    fill_table(2, (0, 1))
    fill_table(3, (0, 1, 2))

    def gather(level, windows):
        rows = jnp.concatenate([ref[...] for _, ref in windows], axis=0)
        pick = []
        for step, ref in windows:
            shape = (24, ref.shape[0])
            out_row = iota(shape, 0)
            spot = places(jnp.bitwise_and(out_row, 7))[level] - GROUPS * step
            spot = GROUPS - 1 - spot if level < 2 else spot
            inside = jnp.logical_and(spot >= 0, spot < GROUPS)
            want = 3 * spot + jnp.right_shift(out_row, 3)
            hit = jnp.logical_and(inside, iota(shape, 1) == want)
            pick.append(jnp.where(hit, 1.0, 0.0))
        zbuf[level] = pick_rows(jnp.concatenate(pick, axis=1), rows)

    def put(first_row, span, fold, even, odd):
        pair = jnp.concatenate([even, odd], axis=0).astype(BF16)
        target = folds if fold else cols
        target[first_row : first_row + 16, pl.ds(span, 128)] = pair

    def rounded(value):
        return value.astype(BF16).astype(F32)

    def put_sum(first_row, span, fold, value):
        high = rounded(value)
        put(first_row, span, fold, high, value - high)

    def columns(rate, levels):
        @pl.loop(0, CHUNKS)
        def _(chunk):
            span = pl.multiple_of(chunk * 128, 128)

            def soft(level):
                z = [zbuf[level, 8 * k : 8 * k + 8, pl.ds(span, 128)] for k in range(3)]
                if rate is not None:
                    q = [qbuf[level, 8 * k : 8 * k + 8, pl.ds(span, 128)] for k in range(4)]
                    z = [z[k] + rate * (q[k + 1] - q[0]) for k in range(3)]
                z = [jnp.zeros((8, 128), F32)] + z
                top = jnp.maximum(jnp.maximum(z[0], z[1]), jnp.maximum(z[2], z[3]))
                e = [jnp.exp(x - top) for x in z]
                inv = 1.0 / ((e[0] + e[1]) + (e[2] + e[3]))
                return [x * inv for x in e]

            def inner(level, values):
                return sum(table[2, level, k] * values[k] for k in range(4))

            def both(level, values, sign):
                show = [values[k] * table[0, level, k] for k in range(4)]
                fold = [values[k] * table[1, level, k] for k in range(4)]
                return show, [-x for x in fold] if sign < 0 else fold

            def put_slots(first_row, pairs):
                for fold, values in enumerate(pairs):
                    put(first_row, span, fold, values[0], values[1])
                    put(first_row + 16, span, fold, values[2], values[3])

            def put_sums(first_row, pairs):
                for fold, values in enumerate(pairs):
                    put_sum(first_row, span, fold, sum(rounded(x) for x in values))

            one = reach1[:, pl.ds(span, 128)]
            two = reach2[:, pl.ds(span, 128)]
            if 0 in levels and rate is None:
                put_slots(0, both(0, [two] * 4, 1))
            if 0 in levels:
                x1 = one * inner(0, soft(0))
                y1 = [two * s for s in soft(1)]
                y2 = inner(1, y1)
                put_slots(ROW1, both(1, [x1] * 4, -1))
                put_sums(ROW1 + 32, both(1, y1, 1))
                s2 = soft(2)
                x2 = [x1 * s for s in s2]
                x3 = inner(2, x2)
                put_slots(ROW2, both(2, [y2] * 4, 1))
                put_sums(ROW2 + 32, both(2, x2, -1))
                for k in range(4):
                    strat[0, 8 * k : 8 * k + 8, pl.ds(span, 128)] = s2[k]
            if 3 not in levels:
                hold[0, :, pl.ds(span, 128)] = x3
                hold[1, :, pl.ds(span, 128)] = y2
                return
            if 0 not in levels:
                x3 = hold[0, :, pl.ds(span, 128)]
                y2 = hold[1, :, pl.ds(span, 128)]
            s3 = soft(3)
            y3 = [y2 * s for s in s3]
            put_slots(ROW3, both(3, [x3] * 4, -1))
            put_sums(ROW3 + 32, both(3, y3, 1))
            for k in range(4):
                strat[1, 8 * k : 8 * k + 8, pl.ds(span, 128)] = s3[k]

    def payoffs(top, end):
        sums = jnp.dot(folds[top:end, :], cards_tv[...], preferred_element_type=F32)
        for part, value in enumerate(three_parts(sums)):
            cols[top:end, PAD + 64 * part : PAD + 64 * part + 64] = value
        for first in range(0, PAD, 256):
            last = min(first + 256, PAD)
            pay[top:end, first:last] = jnp.dot(
                cols[top:end, :], blocks[:, first:last], preferred_element_type=F32
            )

    def values_up(last):
        def step(chunk, total):
            span = pl.multiple_of(chunk * 128, 128)
            lively = 1.0 - dead_p[:, pl.ds(span, 128)]

            def pair(first_row):
                fold = folds[first_row : first_row + 16, pl.ds(span, 128)].astype(F32)
                both = pay[first_row : first_row + 16, pl.ds(span, 128)] + fold * lively
                return [both[0:8], both[8:16]]

            def slots(first_row):
                return pair(first_row) + pair(first_row + 16)

            def summed(first_row):
                return sum(pair(first_row))

            def weighted(which, values):
                return sum(
                    strat[which, 8 * k : 8 * k + 8, pl.ds(span, 128)] * values[k]
                    for k in range(4)
                )

            def joined(level, values, below):
                return [values[k] + table[2, level, k] * below for k in range(4)]

            q3 = slots(ROW3)
            q2 = joined(2, slots(ROW2), summed(ROW3 + 32))
            q1 = joined(1, slots(ROW1), summed(ROW2 + 32) + weighted(1, q3))
            q0 = joined(0, slots(0), summed(ROW1 + 32) + weighted(0, q2))
            for level, q in enumerate((q0, q1, q2, q3)):
                if last:
                    for k in (0, 2):
                        for half in (0, 4):
                            rows = jnp.concatenate([q[k][half : half + 4], q[k + 1][half : half + 4]], axis=0)
                            top = 4 * half + 4 * k
                            qsend[level, top : top + 8, pl.ds(span, 128)] = rows
                else:
                    for k in range(4):
                        qbuf[level, 8 * k : 8 * k + 8, pl.ds(span, 128)] = q[k]
                total = total + ((q[0] * q[0] + q[1] * q[1]) + (q[2] * q[2] + q[3] * q[3]))
            return total

        total = lax.fori_loop(0, CHUNKS, step, jnp.zeros((8, 128), F32))
        return jnp.sum(total, axis=0, keepdims=True)

    def exchange(src, ring, count, send_sem, recv_sem, peer):
        def copy(j):
            return pltpu.make_async_remote_copy(
                src_ref=src,
                dst_ref=ring.at[j],
                send_sem=send_sem.at[j],
                recv_sem=recv_sem.at[j],
                device_id=peer(j),
                device_id_type=MESH,
            )

        copies = [copy(j) for j in sorted(range(1, count), key=lambda j: -min(j, count - j))]
        for item in copies:
            item.start()

        def finish():
            for item in reversed(copies):
                item.wait()

        return finish

    def reduce_start(total, ring_a, recv_a):
        part_a[...] = total
        ring_a[0] = total
        return exchange(part_a, ring_a, PEERS_A, ar_send_a, recv_a, peer_a)

    def reduce_second(finish, ring_a, ring_b, recv_b):
        finish()
        total = jnp.sum(ring_a[...], axis=0)
        part_b[...] = total
        ring_b[0] = total
        return exchange(part_b, ring_b, CHIPS, ar_send_b, recv_b, peer_b)

    def reduce_rate(finish, ring_b):
        finish()
        total = jnp.sum(jnp.sum(ring_b[...], axis=0), axis=1, keepdims=True)
        return jnp.broadcast_to(STEP_SCALE / jnp.sqrt(total / ENTRIES + EPS), (8, 128))

    sends[0].wait()
    gather(1, [(0, diffs.at[1]), (-1, win1)])
    sends[1].wait()
    sends[2].wait()
    gather(0, [(0, diffs.at[0]), (-1, win0a), (-2, win0b)])
    heard(1)
    announce(2)
    sends[3].wait()
    gather(2, [(0, diffs.at[2]), (1, win2)])
    columns(None, (0, 1, 2))
    heard(2)
    announce(3)
    payoffs(0, ROW3)
    sends[4].wait()
    sends[5].wait()
    gather(3, [(0, diffs.at[3]), (1, win3a), (2, win3b)])
    columns(None, (3,))
    payoffs(ROW3, ROWS)
    heard(3)
    first = reduce_start(values_up(False), ring_a1, ar_recv_a1)
    rate = reduce_rate(reduce_second(first, ring_a1, ring_b1, ar_recv_b1), ring_b1)
    columns(rate, (0, 1, 2, 3))
    payoffs(ROW1, ROWS)
    first = reduce_start(values_up(True), ring_a2, ar_recv_a2)

    def back(idx, src, dst, step):
        return pltpu.make_async_remote_copy(
            src_ref=src,
            dst_ref=dst,
            send_sem=ret_send.at[idx],
            recv_sem=ret_recv.at[idx],
            device_id=at_node(step),
            device_id_type=MESH,
        )

    backs = [
        back(0, qsend.at[3], ret3a, 1),
        back(1, qsend.at[3, pl.ds(0, 16)], ret3b, 2),
        back(2, qsend.at[2, pl.ds(0, 16)], ret2, 1),
        back(3, qsend.at[0], ret0a, -1),
        back(4, qsend.at[0, pl.ds(16, 16)], ret0b, -2),
        back(5, qsend.at[1, pl.ds(16, 16)], ret1, -1),
    ]
    for copy in backs:
        copy.start()
    second = reduce_second(first, ring_a2, ring_b2, ar_recv_b2)

    def scatter(level, windows):
        rows = jnp.concatenate([ref[...] for _, _, ref in windows], axis=0)
        pick = []
        for step, half, ref in windows:
            shape = (SLOT_DEV, ref.shape[0])
            out_row = iota(shape, 0)
            col = iota(shape, 1) + 16 * half
            chain = 4 * jnp.right_shift(col, 4) + jnp.bitwise_and(col, 3)
            same_slot = jnp.bitwise_and(jnp.right_shift(col, 2), 3) == jnp.bitwise_and(out_row, 3)
            spot = places(chain)[level] + GROUPS * step
            hit = jnp.logical_and(same_slot, spot == jnp.right_shift(out_row, 2))
            pick.append(jnp.where(hit, 1.0, 0.0))
        out_values[0, level] = pick_rows(jnp.concatenate(pick, axis=1), rows)[:, 0:HANDS]

    backs[5].wait()
    scatter(1, [(0, 0, qsend.at[1]), (1, 1, ret1)])
    backs[3].wait()
    backs[4].wait()
    scatter(0, [(0, 0, qsend.at[0]), (1, 0, ret0a), (2, 1, ret0b)])
    backs[2].wait()
    scatter(2, [(0, 0, qsend.at[2]), (-1, 0, ret2)])
    backs[0].wait()
    backs[1].wait()
    scatter(3, [(0, 0, qsend.at[3]), (-1, 0, ret3a), (-2, 0, ret3b)])
    rate = reduce_rate(second, ring_b2)
    for level in range(LEVELS):
        out_logits[0, level] = own[level] + rate[0:1, 0:1] * out_values[0, level]


def per_device(
    logits, pot_size, node_type, parent_slot, range_one, range_two, hand_rank, live_mask
):
    small = (LEVELS, SLOT_DEV)
    rows = (SLOT_DEV, HANDS)
    wide = (SLOT_DEV, PAD)
    vmem = pltpu.VMEM
    dma = pltpu.SemaphoreType.DMA
    scratch = [
        vmem((LEVELS,) + rows, F32),
        vmem(small, F32),
        vmem(small, jnp.int32),
        pltpu.SMEM(small, jnp.int32),
        vmem((1, HANDS), F32),
        vmem((1, HANDS), F32),
        vmem((1, HANDS), jnp.int32),
        vmem((1, HANDS), jnp.int32),
        vmem((64, PAD), F32),
        vmem((PAD, 64), BF16),
        vmem((LEVELS, 24, PAD), F32),
        vmem((24, PAD), F32),
        vmem((16, PAD), F32),
        vmem((16, PAD), F32),
        vmem((16, PAD), F32),
        vmem((24, PAD), F32),
        vmem((8, PAD), F32),
        vmem((4,) + small, F32),
        vmem((4,) + small, jnp.int32),
        vmem((1, PAD), F32),
        vmem((1, PAD), F32),
        vmem((1, PAD), F32),
        vmem((1, PAD), F32),
        vmem((64, PAD), BF16),
        vmem((3, LEVELS, 4, 8, 128), F32),
        vmem((LEVELS, 24, PAD), F32),
        vmem((2,) + wide, F32),
        vmem((LEVELS,) + wide, F32),
        vmem((LEVELS,) + wide, F32),
        vmem((ROWS, DEEP), BF16),
        vmem((ROWS, PAD), BF16),
        vmem((DEEP, PAD), BF16),
        vmem((ROWS, PAD), F32),
        vmem((1, 128), F32),
        vmem((1, 128), F32),
        vmem((PEERS_A, 1, 128), F32),
        vmem((CHIPS, 1, 128), F32),
        vmem((PEERS_A, 1, 128), F32),
        vmem((CHIPS, 1, 128), F32),
        vmem(wide, F32),
        vmem((16, PAD), F32),
        vmem((16, PAD), F32),
        vmem((16, PAD), F32),
        vmem(wide, F32),
        vmem((16, PAD), F32),
        vmem((2, 8, PAD), F32),
        pltpu.SemaphoreType.REGULAR((4,)),
        dma((10,)),
        dma((14,)),
        dma((14,)),
        dma((6,)),
        dma((6,)),
        dma((PEERS_A,)),
        dma((CHIPS,)),
        dma((PEERS_A,)),
        dma((CHIPS,)),
        dma((PEERS_A,)),
        dma((CHIPS,)),
    ]
    whole = jax.ShapeDtypeStruct(logits.shape, F32)
    free = pl.BlockSpec(memory_space=pl.ANY)
    table = card_rows()
    turned = table.T.copy()
    turned[:, CARDS] = 1.0
    return pl.pallas_call(
        kernel,
        name="extragradient",
        out_shape=(whole, whole),
        in_specs=[free] * 10,
        out_specs=(pl.BlockSpec(memory_space=pltpu.VMEM),) * 2,
        scratch_shapes=scratch,
        compiler_params=pltpu.CompilerParams(
            collective_id=0, has_side_effects=True, vmem_limit_bytes=40 * 1024 * 1024
        ),
    )(
        *[
            pltpu.with_memory_space_constraint(value, pltpu.HBM)
            for value in (
                logits,
                pot_size,
                node_type,
                parent_slot,
                range_one,
                range_two,
                hand_rank,
                live_mask,
                jnp.asarray(table),
                jnp.asarray(turned, BF16),
            )
        ]
    )


def solution(mesh):
    placed = (
        P("board", None, "node", None),
        P(None, "node"),
        P(None, "node"),
        P(None, "node"),
        P("board", None),
        P("board", None),
        P("board", None),
        P("board", None),
    )
    return jax.shard_map(
        per_device,
        mesh=mesh,
        in_specs=placed,
        out_specs=(P("board", None, "node", None), P("board", None, "node", None)),
        check_vma=False,
    )
```

```python
import functools

import jax
import jax.numpy as jnp
import numpy as np
from jax import lax
from jax.experimental import pallas as pl
from jax.experimental.pallas import tpu as pltpu
from jax.sharding import PartitionSpec as P

HANDS = 1326
PAD = 1408
CHUNKS = PAD // 128
LEVELS = 4
SLOT_DEV = 32
GROUPS = SLOT_DEV // 4
NODES = 64
BOARDS = 8
ALL_GROUPS = NODES * GROUPS
ENTRIES = BOARDS * LEVELS * NODES * SLOT_DEV * HANDS
STEP_SCALE = 0.5
EPS = 1e-06
CHIPS = NODES // 2
PEERS_A = 2 * BOARDS
ROW0, SUM1, ROW2, ROW1, SUM2, ROW3, SUM3, ROWS = 0, 32, 48, 80, 112, 128, 160, 176
F32 = jnp.float32
BF16 = jnp.bfloat16
MESH = pl.DeviceIdType.MESH


KEEP_A = 5
CARDS = 52
DEEP = PAD + 3 * 64


def card_rows():
    table = np.zeros((64, PAD), np.float32)
    hand = 0
    for low in range(52):
        for high in range(low + 1, 52):
            if hand < HANDS:
                table[low, hand] = 1.0
                table[high, hand] = 1.0
                hand += 1
    return table


def iota(shape, dim):
    return lax.broadcasted_iota(jnp.int32, shape, dim)


def three_parts(value):
    high = value.astype(BF16)
    rest = value - high.astype(F32)
    mid = rest.astype(BF16)
    return [high, mid, (rest - mid.astype(F32)).astype(BF16)]


def pick_rows(pick, rows):
    parts = jnp.concatenate(three_parts(rows), axis=0)
    pick = jnp.concatenate([pick, pick, pick], axis=1).astype(BF16)
    return jnp.dot(pick, parts, preferred_element_type=F32)


def third(value):
    return jnp.right_shift(value * 43, 7)


def kernel(
    logits,
    pot,
    kind,
    parent,
    range_one,
    range_two,
    rank,
    live,
    cards,
    cards_t,
    out_logits,
    out_values,
    own,
    own_pot,
    own_kind,
    parent_s,
    rng1,
    rng2,
    rank_v,
    live_v,
    cards_v,
    cards_tv,
    diffs,
    win0a,
    win0b,
    win1,
    win2,
    win3a,
    win3b,
    near_pot,
    near_kind,
    reach1,
    reach2,
    rank_p,
    dead_p,
    rhs_cards,
    table,
    zbuf,
    strat,
    qbuf,
    qsend,
    cols,
    folds,
    blocks,
    pay,
    part_a,
    part_b,
    ring_a1,
    ring_b1,
    ring_a2,
    ring_b2,
    ret0a,
    ret0b,
    ret1,
    ret2,
    ret3a,
    ret3b,
    hold,
    known_node,
    known_board,
    in_sem,
    halo_send,
    halo_recv,
    ret_send,
    ret_recv,
    ar_send_a,
    ar_send_b,
    ar_recv_a1,
    ar_recv_b1,
    ar_recv_a2,
    ar_recv_b2,
):
    node = lax.axis_index("node")
    board = lax.axis_index("board")
    core = lax.rem(node, 2)
    chip = node // 2

    def at_node(step):
        return {"node": lax.rem(node + step + NODES, NODES), "board": board}

    def at_board(step):
        return {"node": node, "board": lax.rem(board + step + BOARDS, BOARDS)}

    def peer_a(j):
        spot = lax.rem(board * 2 + core + j, PEERS_A)
        return {"node": chip * 2 + lax.rem(spot, 2), "board": spot // 2}

    def peer_b(j):
        return {"node": lax.rem(chip + j, CHIPS) * 2 + core, "board": board}

    loads = [
        pltpu.make_async_copy(src, dst, in_sem.at[idx])
        for idx, (src, dst) in enumerate(
            [
                (logits.at[0], own),
                (live, live_v),
                (rank, rank_v),
                (cards, cards_v),
                (cards_t, cards_tv),
                (pot, own_pot),
                (kind, own_kind),
                (parent, parent_s),
                (range_one, rng1),
                (range_two, rng2),
            ]
        )
    ]

    barrier = pltpu.get_barrier_semaphore()
    close = [at_node(step) for step in (1, -1, 2, -2)]
    if BOARDS > 1:
        close += [at_board(step) for step in (1, -1)]
    loads[0].start()
    for peer in close:
        pl.semaphore_signal(barrier, inc=1, device_id=peer, device_id_type=MESH)
    for load in loads[1:]:
        load.start()
    along_node = []
    step = 1
    while step < CHIPS // 2:
        along_node.append([at_node(2 * step), at_node(-2 * step)])
        step *= 2
    along_board = []
    step = 1
    while step <= BOARDS // 2:
        along_board.append([at_board(step), at_board(-step)][: 1 if 2 * step == BOARDS else 2])
        step *= 2

    def announce(idx, rounds, known):
        if idx < len(rounds):
            for peer in rounds[idx]:
                pl.semaphore_signal(known.at[idx], inc=1, device_id=peer, device_id_type=MESH)

    def heard(idx, rounds, known):
        if idx < len(rounds):
            pl.semaphore_wait(known.at[idx], len(rounds[idx]))

    def next_round(idx):
        heard(idx, along_node, known_node)
        heard(idx, along_board, known_board)
        announce(idx + 1, along_node, known_node)
        announce(idx + 1, along_board, known_board)

    def halo(idx, src, dst, step):
        return pltpu.make_async_remote_copy(
            src_ref=src,
            dst_ref=dst,
            send_sem=halo_send.at[idx],
            recv_sem=halo_recv.at[idx],
            device_id=at_node(step),
            device_id_type=MESH,
        )

    halos = []
    for spot, step in enumerate((1, -1, 2, -2)):
        halos.append(halo(2 * spot, pot, near_pot.at[spot], step))
        halos.append(halo(2 * spot + 1, kind, near_kind.at[spot], step))
    sends = [
        halo(8, diffs.at[1, pl.ds(0, 16)], win1, 1),
        halo(9, diffs.at[0], win0a, 1),
        halo(10, diffs.at[0, pl.ds(0, 8)], win0b, 2),
        halo(11, diffs.at[2, pl.ds(0, 16)], win2, -1),
        halo(12, diffs.at[3], win3a, -1),
        halo(13, diffs.at[3, pl.ds(0, 16)], win3b, -2),
    ]
    loads[0].wait()

    out_row = iota((24, SLOT_DEV), 0)
    col = iota((24, SLOT_DEV), 1)
    for level in range(LEVELS):
        group = third(out_row)
        slot = out_row - 3 * group + 1
        group = GROUPS - 1 - group if level < 2 else group
        pick = jnp.where(col == 4 * group + slot, 1.0, jnp.where(col == 4 * group, -1.0, 0.0))
        diffs[level, :, 0:HANDS] = pick_rows(pick, own[level])
        diffs[level, :, HANDS:PAD] = jnp.zeros((24, PAD - HANDS), F32)
    pl.semaphore_wait(barrier, len(close))
    for copy in halos + sends:
        copy.start()
    announce(0, along_node, known_node)
    announce(0, along_board, known_board)
    for load in loads[1:]:
        load.wait()

    zero_row = jnp.zeros((1, PAD), F32)
    reach1[...] = zero_row
    reach2[...] = zero_row
    rank_p[...] = zero_row
    alive = jnp.where(live_v[...] > 0, 1.0, 0.0)
    reach1[:, 0:HANDS] = rng1[...] * alive
    reach2[:, 0:HANDS] = rng2[...] * alive
    rank_p[:, 0:HANDS] = rank_v[...].astype(F32)
    dead_p[...] = jnp.ones((1, PAD), F32)
    dead_p[:, 0:HANDS] = 1.0 - alive
    dead = dead_p[...]
    row = iota((16, PAD), 0)
    head = cards_v[0:48]
    tail = cards_v[48:64]
    rhs_cards[0:48] = head.astype(BF16)
    rhs_cards[48:64] = jnp.where(row == CARDS - 48, dead, tail).astype(BF16)
    lively = 1.0 - dead
    for part in range(3):
        top = PAD + 64 * part
        blocks[top : top + 48] = (-head * lively).astype(BF16)
        blocks[top + 48 : top + 64] = jnp.where(row == CARDS - 48, lively, -tail * lively).astype(BF16)

    @pl.loop(0, CHUNKS)
    def _(jb):
        base = pl.multiple_of(jb * 128, 128)
        rank_j = jnp.broadcast_to(rank_p[:, pl.ds(base, 128)], (128, 128)).T
        mine = cards_tv[pl.ds(base, 128)]
        for first in range(0, PAD, 256):
            last = min(first + 256, PAD)
            shared = jnp.dot(mine, rhs_cards[:, first:last], preferred_element_type=F32)
            for start in range(first, last, 128):
                span = slice(start, start + 128)
                keep = shared[:, start - first : start - first + 128] < 0.5
                order = jnp.clip(rank_p[:, span] - rank_j, -1.0, 1.0)
                blocks[pl.ds(base, 128), span] = jnp.where(keep, order, 0.0).astype(BF16)

    def offset(level):
        return jnp.bitwise_and(node * GROUPS - parent_s[level, 0] // 4 + ALL_GROUPS, ALL_GROUPS - 1)

    off1 = offset(1)
    off2 = offset(2)
    off3 = offset(3)

    def places(spot):
        chain = jnp.bitwise_and(spot + 1, GROUPS - 1)
        late = jnp.logical_and(chain >= KEEP_A, chain + off2 >= GROUPS)
        first = jnp.where(late, chain - GROUPS, chain)
        return [first - off1, first, first + off2, first + off2 + off3]

    next_round(0)
    for copy in halos:
        copy.wait()

    lane = iota((8, SLOT_DEV), 1)
    spots = places(iota((8, SLOT_DEV), 0))
    near = {1: 1, -1: 0, 2: 3, -2: 2}

    def fill_table(level, steps):
        for k in range(4):
            pots = jnp.zeros((8, SLOT_DEV), F32)
            kinds = jnp.zeros((8, SLOT_DEV), F32)
            for step in steps:
                pot_row = own_pot[level : level + 1] if step == 0 else near_pot[near[step], level : level + 1]
                kind_row = own_kind[level : level + 1] if step == 0 else near_kind[near[step], level : level + 1]
                hit = lane + SLOT_DEV * step == 4 * spots[level] + k
                pots += jnp.where(hit, pot_row, 0.0)
                kinds += jnp.where(hit, kind_row.astype(F32), 0.0)
            pots = jnp.broadcast_to(jnp.sum(pots, axis=1, keepdims=True), (8, 128))
            kinds = jnp.broadcast_to(jnp.sum(kinds, axis=1, keepdims=True), (8, 128))
            sign = -1.0 if level % 2 == 0 else 1.0
            table[0, level, k] = jnp.where(kinds > 1.5, pots, 0.0)
            table[1, level, k] = jnp.where(jnp.abs(kinds - 1.0) < 0.5, pots, 0.0) * sign
            table[2, level, k] = jnp.where(kinds < 0.5, 1.0, 0.0)

    fill_table(0, (-2, -1, 0))
    fill_table(1, (-1, 0))
    fill_table(2, (0, 1))
    fill_table(3, (0, 1, 2))

    def gather(level, windows):
        rows = jnp.concatenate([ref[...] for _, ref in windows], axis=0)
        pick = []
        for step, ref in windows:
            shape = (24, ref.shape[0])
            out_row = iota(shape, 0)
            spot = places(jnp.bitwise_and(out_row, 7))[level] - GROUPS * step
            spot = GROUPS - 1 - spot if level < 2 else spot
            inside = jnp.logical_and(spot >= 0, spot < GROUPS)
            want = 3 * spot + jnp.right_shift(out_row, 3)
            hit = jnp.logical_and(inside, iota(shape, 1) == want)
            pick.append(jnp.where(hit, 1.0, 0.0))
        zbuf[level] = pick_rows(jnp.concatenate(pick, axis=1), rows)

    def put(first_row, span, fold, even, odd):
        pair = jnp.concatenate([even, odd], axis=0).astype(BF16)
        target = folds if fold else cols
        target[first_row : first_row + 16, pl.ds(span, 128)] = pair

    def rounded(value):
        return value.astype(BF16).astype(F32)

    def put_sum(first_row, span, fold, value):
        high = rounded(value)
        put(first_row, span, fold, high, value - high)

    def columns(rate, stages):
        @pl.loop(0, CHUNKS)
        def _(chunk):
            span = pl.multiple_of(chunk * 128, 128)

            def soft(level):
                z = [zbuf[level, 8 * k : 8 * k + 8, pl.ds(span, 128)] for k in range(3)]
                if rate is not None:
                    q = [qbuf[level, 8 * k : 8 * k + 8, pl.ds(span, 128)] for k in range(4)]
                    z = [z[k] + rate * (q[k + 1] - q[0]) for k in range(3)]
                z = [jnp.zeros((8, 128), F32)] + z
                top = jnp.maximum(jnp.maximum(z[0], z[1]), jnp.maximum(z[2], z[3]))
                e = [jnp.exp(x - top) for x in z]
                inv = 1.0 / ((e[0] + e[1]) + (e[2] + e[3]))
                return [x * inv for x in e]

            def inner(level, values):
                return sum(table[2, level, k] * values[k] for k in range(4))

            def both(level, values, sign):
                show = [values[k] * table[0, level, k] for k in range(4)]
                fold = [values[k] * table[1, level, k] for k in range(4)]
                return show, [-x for x in fold] if sign < 0 else fold

            def put_slots(first_row, pairs):
                for fold, values in enumerate(pairs):
                    put(first_row, span, fold, values[0], values[1])
                    put(first_row + 16, span, fold, values[2], values[3])

            def put_sums(first_row, pairs):
                for fold, values in enumerate(pairs):
                    put_sum(first_row, span, fold, sum(rounded(x) for x in values))

            one = reach1[:, pl.ds(span, 128)]
            two = reach2[:, pl.ds(span, 128)]
            if 1 in stages:
                if rate is None:
                    put_slots(ROW0, both(0, [two] * 4, 1))
                y1 = [two * s for s in soft(1)]
                y2 = inner(1, y1)
                put_sums(SUM1, both(1, y1, 1))
                put_slots(ROW2, both(2, [y2] * 4, 1))
                hold[1, :, pl.ds(span, 128)] = y2
            if 2 in stages:
                x1 = one * inner(0, soft(0))
                put_slots(ROW1, both(1, [x1] * 4, -1))
                s2 = soft(2)
                x2 = [x1 * s for s in s2]
                put_sums(SUM2, both(2, x2, -1))
                x3 = inner(2, x2)
                hold[0, :, pl.ds(span, 128)] = x3
                for k in range(4):
                    strat[0, 8 * k : 8 * k + 8, pl.ds(span, 128)] = s2[k]
            if 3 in stages:
                if 2 not in stages:
                    x3 = hold[0, :, pl.ds(span, 128)]
                    y2 = hold[1, :, pl.ds(span, 128)]
                s3 = soft(3)
                y3 = [y2 * s for s in s3]
                put_slots(ROW3, both(3, [x3] * 4, -1))
                put_sums(SUM3, both(3, y3, 1))
                for k in range(4):
                    strat[1, 8 * k : 8 * k + 8, pl.ds(span, 128)] = s3[k]

    def payoffs(top, end, up=None):
        sums = jnp.dot(folds[top:end, :], cards_tv[...], preferred_element_type=F32)
        for part, value in enumerate(three_parts(sums)):
            cols[top:end, PAD + 64 * part : PAD + 64 * part + 64] = value
        total = jnp.zeros((8, 128), F32)
        for first in range(0, PAD, 256):
            last = min(first + 256, PAD)
            pay[top:end, first:last] = jnp.dot(
                cols[top:end, :], blocks[:, first:last], preferred_element_type=F32
            )
            if up is not None:
                for span in range(first, last, 128):
                    total = up(span, total)
        return jnp.sum(total, axis=0, keepdims=True)

    def values_up(last):
        def step(span, total):
            lively = 1.0 - dead_p[:, pl.ds(span, 128)]

            def pair(first_row):
                fold = folds[first_row : first_row + 16, pl.ds(span, 128)].astype(F32)
                both = pay[first_row : first_row + 16, pl.ds(span, 128)] + fold * lively
                return [both[0:8], both[8:16]]

            def slots(first_row):
                return pair(first_row) + pair(first_row + 16)

            def summed(first_row):
                return sum(pair(first_row))

            def weighted(which, values):
                return sum(
                    strat[which, 8 * k : 8 * k + 8, pl.ds(span, 128)] * values[k]
                    for k in range(4)
                )

            def joined(level, values, below):
                return [values[k] + table[2, level, k] * below for k in range(4)]

            q3 = slots(ROW3)
            q2 = joined(2, slots(ROW2), summed(SUM3))
            q1 = joined(1, slots(ROW1), summed(SUM2) + weighted(1, q3))
            q0 = joined(0, slots(ROW0), summed(SUM1) + weighted(0, q2))
            for level, q in enumerate((q0, q1, q2, q3)):
                if last:
                    for k in (0, 2):
                        for half in (0, 4):
                            rows = jnp.concatenate([q[k][half : half + 4], q[k + 1][half : half + 4]], axis=0)
                            top = 4 * half + 4 * k
                            qsend[level, top : top + 8, pl.ds(span, 128)] = rows
                else:
                    for k in range(4):
                        qbuf[level, 8 * k : 8 * k + 8, pl.ds(span, 128)] = q[k]
                total = total + ((q[0] * q[0] + q[1] * q[1]) + (q[2] * q[2] + q[3] * q[3]))
            return total

        return step

    def exchange(src, ring, count, send_sem, recv_sem, peer):
        def copy(j):
            return pltpu.make_async_remote_copy(
                src_ref=src,
                dst_ref=ring.at[j],
                send_sem=send_sem.at[j],
                recv_sem=recv_sem.at[j],
                device_id=peer(j),
                device_id_type=MESH,
            )

        copies = [copy(j) for j in sorted(range(1, count), key=lambda j: -min(j, count - j))]
        for item in copies:
            item.start()

        def finish():
            for item in reversed(copies):
                item.wait()

        return finish

    def reduce_start(total, ring_a, recv_a):
        part_a[...] = total
        ring_a[0] = total
        return exchange(part_a, ring_a, PEERS_A, ar_send_a, recv_a, peer_a)

    def reduce_second(finish, ring_a, ring_b, recv_b, ready=None):
        finish()
        if ready is not None:
            ready()
        total = jnp.sum(ring_a[...], axis=0)
        part_b[...] = total
        ring_b[0] = total
        return exchange(part_b, ring_b, CHIPS, ar_send_b, recv_b, peer_b)

    def reduce_rate(finish, ring_b):
        finish()
        total = jnp.sum(jnp.sum(ring_b[...], axis=0), axis=1, keepdims=True)
        return jnp.broadcast_to(STEP_SCALE / jnp.sqrt(total / ENTRIES + EPS), (8, 128))

    sends[0].wait()
    gather(1, [(0, diffs.at[1]), (-1, win1)])
    columns(None, (1,))
    next_round(1)
    payoffs(ROW0, ROW1)
    heard(2, along_node, known_node)
    announce(3, along_node, known_node)
    for copy in sends[1:4]:
        copy.wait()
    gather(0, [(0, diffs.at[0]), (-1, win0a), (-2, win0b)])
    gather(2, [(0, diffs.at[2]), (1, win2)])
    columns(None, (2,))
    sends[4].wait()
    sends[5].wait()
    gather(3, [(0, diffs.at[3]), (1, win3a), (2, win3b)])
    columns(None, (3,))
    total = payoffs(ROW1, ROWS, values_up(False))
    heard(2, along_board, known_board)
    first = reduce_start(total, ring_a1, ar_recv_a1)
    ready = functools.partial(heard, 3, along_node, known_node)
    rate = reduce_rate(reduce_second(first, ring_a1, ring_b1, ar_recv_b1, ready), ring_b1)
    columns(rate, (1, 2, 3))
    total = payoffs(SUM1, ROWS, values_up(True))
    first = reduce_start(total, ring_a2, ar_recv_a2)

    def back(idx, src, dst, step):
        return pltpu.make_async_remote_copy(
            src_ref=src,
            dst_ref=dst,
            send_sem=ret_send.at[idx],
            recv_sem=ret_recv.at[idx],
            device_id=at_node(step),
            device_id_type=MESH,
        )

    backs = [
        back(0, qsend.at[3], ret3a, 1),
        back(1, qsend.at[3, pl.ds(0, 16)], ret3b, 2),
        back(2, qsend.at[2, pl.ds(0, 16)], ret2, 1),
        back(3, qsend.at[0], ret0a, -1),
        back(4, qsend.at[0, pl.ds(16, 16)], ret0b, -2),
        back(5, qsend.at[1, pl.ds(16, 16)], ret1, -1),
    ]
    for copy in backs:
        copy.start()
    second = reduce_second(first, ring_a2, ring_b2, ar_recv_b2)

    def scatter(level, windows):
        rows = jnp.concatenate([ref[...] for _, _, ref in windows], axis=0)
        pick = []
        for step, half, ref in windows:
            shape = (SLOT_DEV, ref.shape[0])
            out_row = iota(shape, 0)
            col = iota(shape, 1) + 16 * half
            chain = 4 * jnp.right_shift(col, 4) + jnp.bitwise_and(col, 3)
            same_slot = jnp.bitwise_and(jnp.right_shift(col, 2), 3) == jnp.bitwise_and(out_row, 3)
            spot = places(chain)[level] + GROUPS * step
            hit = jnp.logical_and(same_slot, spot == jnp.right_shift(out_row, 2))
            pick.append(jnp.where(hit, 1.0, 0.0))
        out_values[0, level] = pick_rows(jnp.concatenate(pick, axis=1), rows)[:, 0:HANDS]

    backs[5].wait()
    scatter(1, [(0, 0, qsend.at[1]), (1, 1, ret1)])
    backs[3].wait()
    backs[4].wait()
    scatter(0, [(0, 0, qsend.at[0]), (1, 0, ret0a), (2, 1, ret0b)])
    backs[2].wait()
    scatter(2, [(0, 0, qsend.at[2]), (-1, 0, ret2)])
    backs[0].wait()
    backs[1].wait()
    scatter(3, [(0, 0, qsend.at[3]), (-1, 0, ret3a), (-2, 0, ret3b)])
    rate = reduce_rate(second, ring_b2)
    for level in range(LEVELS):
        out_logits[0, level] = own[level] + rate[0:1, 0:1] * out_values[0, level]


def write_out(logits_v, values_v, out_logits, out_values, sem):
    copies = [
        pltpu.make_async_copy(logits_v, out_logits, sem.at[0]),
        pltpu.make_async_copy(values_v, out_values, sem.at[1]),
    ]
    for copy in copies:
        copy.start()
    for copy in copies:
        copy.wait()


def per_device(
    logits, pot_size, node_type, parent_slot, range_one, range_two, hand_rank, live_mask
):
    small = (LEVELS, SLOT_DEV)
    rows = (SLOT_DEV, HANDS)
    wide = (SLOT_DEV, PAD)
    vmem = pltpu.VMEM
    dma = pltpu.SemaphoreType.DMA
    scratch = [
        vmem((LEVELS,) + rows, F32),
        vmem(small, F32),
        vmem(small, jnp.int32),
        pltpu.SMEM(small, jnp.int32),
        vmem((1, HANDS), F32),
        vmem((1, HANDS), F32),
        vmem((1, HANDS), jnp.int32),
        vmem((1, HANDS), jnp.int32),
        vmem((64, PAD), F32),
        vmem((PAD, 64), BF16),
        vmem((LEVELS, 24, PAD), F32),
        vmem((24, PAD), F32),
        vmem((8, PAD), F32),
        vmem((16, PAD), F32),
        vmem((16, PAD), F32),
        vmem((24, PAD), F32),
        vmem((16, PAD), F32),
        vmem((4,) + small, F32),
        vmem((4,) + small, jnp.int32),
        vmem((1, PAD), F32),
        vmem((1, PAD), F32),
        vmem((1, PAD), F32),
        vmem((1, PAD), F32),
        vmem((64, PAD), BF16),
        vmem((3, LEVELS, 4, 8, 128), F32),
        vmem((LEVELS, 24, PAD), F32),
        vmem((2,) + wide, F32),
        vmem((LEVELS,) + wide, F32),
        vmem((LEVELS,) + wide, F32),
        vmem((ROWS, DEEP), BF16),
        vmem((ROWS, PAD), BF16),
        vmem((DEEP, PAD), BF16),
        vmem((ROWS, PAD), F32),
        vmem((1, 128), F32),
        vmem((1, 128), F32),
        vmem((PEERS_A, 1, 128), F32),
        vmem((CHIPS, 1, 128), F32),
        vmem((PEERS_A, 1, 128), F32),
        vmem((CHIPS, 1, 128), F32),
        vmem(wide, F32),
        vmem((16, PAD), F32),
        vmem((16, PAD), F32),
        vmem((16, PAD), F32),
        vmem(wide, F32),
        vmem((16, PAD), F32),
        vmem((2, 8, PAD), F32),
        pltpu.SemaphoreType.REGULAR((4,)),
        pltpu.SemaphoreType.REGULAR((3,)),
        dma((10,)),
        dma((14,)),
        dma((14,)),
        dma((6,)),
        dma((6,)),
        dma((PEERS_A,)),
        dma((CHIPS,)),
        dma((PEERS_A,)),
        dma((CHIPS,)),
        dma((PEERS_A,)),
        dma((CHIPS,)),
    ]
    whole = jax.ShapeDtypeStruct(logits.shape, F32)
    free = pl.BlockSpec(memory_space=pl.ANY)
    table = card_rows()
    turned = table.T.copy()
    turned[:, CARDS] = 1.0
    found = pl.pallas_call(
        kernel,
        name="extragradient",
        out_shape=(whole, whole),
        in_specs=[free] * 10,
        out_specs=(pl.BlockSpec(memory_space=pltpu.VMEM),) * 2,
        scratch_shapes=scratch,
        compiler_params=pltpu.CompilerParams(
            collective_id=0, has_side_effects=True, vmem_limit_bytes=40 * 1024 * 1024
        ),
    )(
        *[
            pltpu.with_memory_space_constraint(value, pltpu.HBM)
            for value in (
                logits,
                pot_size,
                node_type,
                parent_slot,
                range_one,
                range_two,
                hand_rank,
                live_mask,
                jnp.asarray(table),
                jnp.asarray(turned, BF16),
            )
        ]
    )
    return pl.pallas_call(
        write_out,
        name="write_out",
        out_shape=(whole, whole),
        in_specs=[free] * 2,
        out_specs=(pl.BlockSpec(memory_space=pltpu.HBM),) * 2,
        scratch_shapes=[dma((2,))],
    )(*[pltpu.with_memory_space_constraint(value, pltpu.VMEM) for value in found])


def solution(mesh):
    placed = (
        P("board", None, "node", None),
        P(None, "node"),
        P(None, "node"),
        P(None, "node"),
        P("board", None),
        P("board", None),
        P("board", None),
        P("board", None),
    )
    return jax.shard_map(
        per_device,
        mesh=mesh,
        in_specs=placed,
        out_specs=(P("board", None, "node", None), P("board", None, "node", None)),
        check_vma=False,
    )
```

```python
import functools

import jax
import jax.numpy as jnp
import numpy as np
from jax import lax
from jax.experimental import pallas as pl
from jax.experimental.pallas import tpu as pltpu
from jax.sharding import PartitionSpec as P

HANDS = 1326
PAD = 1408
CHUNKS = PAD // 128
LEVELS = 4
SLOT_DEV = 32
GROUPS = SLOT_DEV // 4
NODES = 64
BOARDS = 8
ALL_GROUPS = NODES * GROUPS
ENTRIES = BOARDS * LEVELS * NODES * SLOT_DEV * HANDS
STEP_SCALE = 0.5
EPS = 1e-06
CHIPS = NODES // 2
PEERS_A = 2 * BOARDS
ROW0, SUM1, ROW2, ROW1, SUM2, ROW3, SUM3, ROWS = 0, 32, 48, 80, 112, 128, 160, 176
F32 = jnp.float32
BF16 = jnp.bfloat16
MESH = pl.DeviceIdType.MESH


KEEP_A = 5
CARDS = 52
DEEP = PAD + 3 * 64


def card_rows():
    table = np.zeros((64, PAD), np.float32)
    hand = 0
    for low in range(52):
        for high in range(low + 1, 52):
            if hand < HANDS:
                table[low, hand] = 1.0
                table[high, hand] = 1.0
                hand += 1
    return table


def iota(shape, dim):
    return lax.broadcasted_iota(jnp.int32, shape, dim)


def three_parts(value):
    high = value.astype(BF16)
    rest = value - high.astype(F32)
    mid = rest.astype(BF16)
    return [high, mid, (rest - mid.astype(F32)).astype(BF16)]


def pick_rows(pick, rows):
    parts = jnp.concatenate(three_parts(rows), axis=0)
    pick = jnp.concatenate([pick, pick, pick], axis=1).astype(BF16)
    return jnp.dot(pick, parts, preferred_element_type=F32)


def third(value):
    return jnp.right_shift(value * 43, 7)


def kernel(
    logits,
    pot,
    kind,
    parent,
    range_one,
    range_two,
    rank,
    live,
    cards,
    cards_t,
    out_logits,
    out_values,
    own,
    own_pot,
    own_kind,
    parent_s,
    rng1,
    rng2,
    rank_v,
    live_v,
    cards_v,
    cards_tv,
    diffs,
    win0a,
    win0b,
    win1,
    win2,
    win3a,
    win3b,
    near_pot,
    near_kind,
    reach1,
    reach2,
    rank_p,
    dead_p,
    rhs_cards,
    table,
    zbuf,
    strat,
    qbuf,
    qsend,
    cols,
    folds,
    blocks,
    pay,
    part_a,
    part_b,
    ring_a1,
    ring_b1,
    ring_a2,
    ring_b2,
    ret0a,
    ret0b,
    ret1,
    ret2,
    ret3a,
    ret3b,
    hold,
    known_node,
    known_board,
    in_sem,
    halo_send,
    halo_recv,
    ret_send,
    ret_recv,
    ar_send_a,
    ar_send_b,
    ar_recv_a1,
    ar_recv_b1,
    ar_recv_a2,
    ar_recv_b2,
):
    node = lax.axis_index("node")
    board = lax.axis_index("board")
    core = lax.rem(node, 2)
    chip = node // 2

    def at_node(step):
        return {"node": lax.rem(node + step + NODES, NODES), "board": board}

    def at_board(step):
        return {"node": node, "board": lax.rem(board + step + BOARDS, BOARDS)}

    def peer_a(j):
        spot = lax.rem(board * 2 + core + j, PEERS_A)
        return {"node": chip * 2 + lax.rem(spot, 2), "board": spot // 2}

    def peer_b(j):
        return {"node": lax.rem(chip + j, CHIPS) * 2 + core, "board": board}

    loads = [
        pltpu.make_async_copy(src, dst, in_sem.at[idx])
        for idx, (src, dst) in enumerate(
            [
                (logits.at[0], own),
                (live, live_v),
                (rank, rank_v),
                (cards, cards_v),
                (cards_t, cards_tv),
                (pot, own_pot),
                (kind, own_kind),
                (parent, parent_s),
                (range_one, rng1),
                (range_two, rng2),
            ]
        )
    ]

    barrier = pltpu.get_barrier_semaphore()
    close = [at_node(step) for step in (1, -1, 2, -2)]
    if BOARDS > 1:
        close += [at_board(step) for step in (1, -1)]
    loads[0].start()
    for peer in close:
        pl.semaphore_signal(barrier, inc=1, device_id=peer, device_id_type=MESH)
    for load in loads[1:]:
        load.start()
    along_node = []
    step = 1
    while step < CHIPS // 2:
        along_node.append([at_node(2 * step), at_node(-2 * step)])
        step *= 2
    along_board = []
    step = 1
    while step <= BOARDS // 2:
        along_board.append([at_board(step), at_board(-step)][: 1 if 2 * step == BOARDS else 2])
        step *= 2

    def announce(idx, rounds, known):
        if idx < len(rounds):
            for peer in rounds[idx]:
                pl.semaphore_signal(known.at[idx], inc=1, device_id=peer, device_id_type=MESH)

    def heard(idx, rounds, known):
        if idx < len(rounds):
            pl.semaphore_wait(known.at[idx], len(rounds[idx]))

    def next_round(idx):
        heard(idx, along_node, known_node)
        heard(idx, along_board, known_board)
        announce(idx + 1, along_node, known_node)
        announce(idx + 1, along_board, known_board)

    def halo(idx, src, dst, step):
        return pltpu.make_async_remote_copy(
            src_ref=src,
            dst_ref=dst,
            send_sem=halo_send.at[idx],
            recv_sem=halo_recv.at[idx],
            device_id=at_node(step),
            device_id_type=MESH,
        )

    halos = []
    for spot, step in enumerate((1, -1, 2, -2)):
        halos.append(halo(2 * spot, pot, near_pot.at[spot], step))
        halos.append(halo(2 * spot + 1, kind, near_kind.at[spot], step))
    sends = [
        halo(8, diffs.at[1, pl.ds(0, 16)], win1, 1),
        halo(9, diffs.at[0], win0a, 1),
        halo(10, diffs.at[0, pl.ds(0, 8)], win0b, 2),
        halo(11, diffs.at[2, pl.ds(0, 16)], win2, -1),
        halo(12, diffs.at[3], win3a, -1),
        halo(13, diffs.at[3, pl.ds(0, 16)], win3b, -2),
    ]
    loads[0].wait()

    out_row = iota((24, SLOT_DEV), 0)
    col = iota((24, SLOT_DEV), 1)
    for level in range(LEVELS):
        group = third(out_row)
        slot = out_row - 3 * group + 1
        group = GROUPS - 1 - group if level < 2 else group
        pick = jnp.where(col == 4 * group + slot, 1.0, jnp.where(col == 4 * group, -1.0, 0.0))
        diffs[level, :, 0:HANDS] = pick_rows(pick, own[level])
        diffs[level, :, HANDS:PAD] = jnp.zeros((24, PAD - HANDS), F32)
    pl.semaphore_wait(barrier, len(close))
    for copy in halos + sends:
        copy.start()
    announce(0, along_node, known_node)
    announce(0, along_board, known_board)
    for load in loads[1:]:
        load.wait()

    zero_row = jnp.zeros((1, PAD), F32)
    reach1[...] = zero_row
    reach2[...] = zero_row
    rank_p[...] = zero_row
    alive = jnp.where(live_v[...] > 0, 1.0, 0.0)
    reach1[:, 0:HANDS] = rng1[...] * alive
    reach2[:, 0:HANDS] = rng2[...] * alive
    rank_p[:, 0:HANDS] = rank_v[...].astype(F32)
    dead_p[...] = jnp.ones((1, PAD), F32)
    dead_p[:, 0:HANDS] = 1.0 - alive
    dead = dead_p[...]
    row = iota((16, PAD), 0)
    head = cards_v[0:48]
    tail = cards_v[48:64]
    rhs_cards[0:48] = head.astype(BF16)
    rhs_cards[48:64] = jnp.where(row == CARDS - 48, dead, tail).astype(BF16)
    lively = 1.0 - dead
    for part in range(3):
        top = PAD + 64 * part
        blocks[top : top + 48] = (-head * lively).astype(BF16)
        blocks[top + 48 : top + 64] = jnp.where(row == CARDS - 48, lively, -tail * lively).astype(BF16)

    for base in range(0, PAD, 128):
        rank_j = jnp.broadcast_to(rank_p[:, pl.ds(base, 128)], (128, 128)).T
        mine = cards_tv[pl.ds(base, 128)]
        for first in range(0, PAD, 256):
            last = min(first + 256, PAD)
            shared = jnp.dot(mine, rhs_cards[:, first:last], preferred_element_type=F32)
            for start in range(first, last, 128):
                span = slice(start, start + 128)
                keep = shared[:, start - first : start - first + 128].astype(BF16) < 0.5
                order = (rank_p[:, span] - rank_j).astype(BF16)
                order = jnp.minimum(jnp.maximum(order, -1.0), 1.0)
                blocks[pl.ds(base, 128), span] = jnp.where(keep, order, 0.0).astype(BF16)

    def offset(level):
        return jnp.bitwise_and(node * GROUPS - parent_s[level, 0] // 4 + ALL_GROUPS, ALL_GROUPS - 1)

    off1 = offset(1)
    off2 = offset(2)
    off3 = offset(3)

    def places(spot):
        chain = jnp.bitwise_and(spot + 1, GROUPS - 1)
        late = jnp.logical_and(chain >= KEEP_A, chain + off2 >= GROUPS)
        first = jnp.where(late, chain - GROUPS, chain)
        return [first - off1, first, first + off2, first + off2 + off3]

    next_round(0)
    for copy in halos:
        copy.wait()

    lane = iota((8, SLOT_DEV), 1)
    spots = places(iota((8, SLOT_DEV), 0))
    near = {1: 1, -1: 0, 2: 3, -2: 2}

    def fill_table(level, steps):
        for k in range(4):
            pots = jnp.zeros((8, SLOT_DEV), F32)
            kinds = jnp.zeros((8, SLOT_DEV), F32)
            for step in steps:
                pot_row = own_pot[level : level + 1] if step == 0 else near_pot[near[step], level : level + 1]
                kind_row = own_kind[level : level + 1] if step == 0 else near_kind[near[step], level : level + 1]
                hit = lane + SLOT_DEV * step == 4 * spots[level] + k
                pots += jnp.where(hit, pot_row, 0.0)
                kinds += jnp.where(hit, kind_row.astype(F32), 0.0)
            pots = jnp.broadcast_to(jnp.sum(pots, axis=1, keepdims=True), (8, 128))
            kinds = jnp.broadcast_to(jnp.sum(kinds, axis=1, keepdims=True), (8, 128))
            sign = -1.0 if level % 2 == 0 else 1.0
            table[0, level, k] = jnp.where(kinds > 1.5, pots, 0.0)
            table[1, level, k] = jnp.where(jnp.abs(kinds - 1.0) < 0.5, pots, 0.0) * sign
            table[2, level, k] = jnp.where(kinds < 0.5, 1.0, 0.0)

    fill_table(0, (-2, -1, 0))
    fill_table(1, (-1, 0))
    fill_table(2, (0, 1))
    fill_table(3, (0, 1, 2))

    def gather(level, windows):
        rows = jnp.concatenate([ref[...] for _, ref in windows], axis=0)
        pick = []
        for step, ref in windows:
            shape = (24, ref.shape[0])
            out_row = iota(shape, 0)
            spot = places(jnp.bitwise_and(out_row, 7))[level] - GROUPS * step
            spot = GROUPS - 1 - spot if level < 2 else spot
            inside = jnp.logical_and(spot >= 0, spot < GROUPS)
            want = 3 * spot + jnp.right_shift(out_row, 3)
            hit = jnp.logical_and(inside, iota(shape, 1) == want)
            pick.append(jnp.where(hit, 1.0, 0.0))
        zbuf[level] = pick_rows(jnp.concatenate(pick, axis=1), rows)

    def put(first_row, span, fold, even, odd):
        pair = jnp.concatenate([even, odd], axis=0).astype(BF16)
        target = folds if fold else cols
        target[first_row : first_row + 16, pl.ds(span, 128)] = pair

    def rounded(value):
        return value.astype(BF16).astype(F32)

    def put_sum(first_row, span, fold, value):
        high = rounded(value)
        put(first_row, span, fold, high, value - high)

    def columns(rate, stages):
        @pl.loop(0, CHUNKS)
        def _(chunk):
            span = pl.multiple_of(chunk * 128, 128)

            def soft(level):
                z = [zbuf[level, 8 * k : 8 * k + 8, pl.ds(span, 128)] for k in range(3)]
                if rate is not None:
                    q = [qbuf[level, 8 * k : 8 * k + 8, pl.ds(span, 128)] for k in range(4)]
                    z = [z[k] + rate * (q[k + 1] - q[0]) for k in range(3)]
                z = [jnp.zeros((8, 128), F32)] + z
                top = jnp.maximum(jnp.maximum(z[0], z[1]), jnp.maximum(z[2], z[3]))
                e = [jnp.exp(x - top) for x in z]
                inv = 1.0 / ((e[0] + e[1]) + (e[2] + e[3]))
                return [x * inv for x in e]

            def inner(level, values):
                return sum(table[2, level, k] * values[k] for k in range(4))

            def both(level, values, sign):
                show = [values[k] * table[0, level, k] for k in range(4)]
                fold = [values[k] * table[1, level, k] for k in range(4)]
                return show, [-x for x in fold] if sign < 0 else fold

            def put_slots(first_row, pairs):
                for fold, values in enumerate(pairs):
                    put(first_row, span, fold, values[0], values[1])
                    put(first_row + 16, span, fold, values[2], values[3])

            def put_sums(first_row, pairs):
                for fold, values in enumerate(pairs):
                    put_sum(first_row, span, fold, sum(rounded(x) for x in values))

            one = reach1[:, pl.ds(span, 128)]
            two = reach2[:, pl.ds(span, 128)]
            if 1 in stages:
                if rate is None:
                    put_slots(ROW0, both(0, [two] * 4, 1))
                y1 = [two * s for s in soft(1)]
                y2 = inner(1, y1)
                put_sums(SUM1, both(1, y1, 1))
                put_slots(ROW2, both(2, [y2] * 4, 1))
                hold[1, :, pl.ds(span, 128)] = y2
            if 2 in stages:
                x1 = one * inner(0, soft(0))
                put_slots(ROW1, both(1, [x1] * 4, -1))
                s2 = soft(2)
                x2 = [x1 * s for s in s2]
                put_sums(SUM2, both(2, x2, -1))
                x3 = inner(2, x2)
                hold[0, :, pl.ds(span, 128)] = x3
                for k in range(4):
                    strat[0, 8 * k : 8 * k + 8, pl.ds(span, 128)] = s2[k]
            if 3 in stages:
                if 2 not in stages:
                    x3 = hold[0, :, pl.ds(span, 128)]
                    y2 = hold[1, :, pl.ds(span, 128)]
                s3 = soft(3)
                y3 = [y2 * s for s in s3]
                put_slots(ROW3, both(3, [x3] * 4, -1))
                put_sums(SUM3, both(3, y3, 1))
                for k in range(4):
                    strat[1, 8 * k : 8 * k + 8, pl.ds(span, 128)] = s3[k]

    def payoffs(top, end, up=None):
        sums = jnp.dot(folds[top:end, :], cards_tv[...], preferred_element_type=F32)
        for part, value in enumerate(three_parts(sums)):
            cols[top:end, PAD + 64 * part : PAD + 64 * part + 64] = value
        total = jnp.zeros((8, 128), F32)
        for first in range(0, PAD, 256):
            last = min(first + 256, PAD)
            pay[top:end, first:last] = jnp.dot(
                cols[top:end, :], blocks[:, first:last], preferred_element_type=F32
            )
            if up is not None:
                for span in range(first, last, 128):
                    total = up(span, total)
        return jnp.sum(total, axis=0, keepdims=True)

    def values_up(last):
        def step(span, total):
            lively = 1.0 - dead_p[:, pl.ds(span, 128)]

            def pair(first_row):
                fold = folds[first_row : first_row + 16, pl.ds(span, 128)].astype(F32)
                both = pay[first_row : first_row + 16, pl.ds(span, 128)] + fold * lively
                return [both[0:8], both[8:16]]

            def slots(first_row):
                return pair(first_row) + pair(first_row + 16)

            def summed(first_row):
                return sum(pair(first_row))

            def weighted(which, values):
                return sum(
                    strat[which, 8 * k : 8 * k + 8, pl.ds(span, 128)] * values[k]
                    for k in range(4)
                )

            def joined(level, values, below):
                return [values[k] + table[2, level, k] * below for k in range(4)]

            q3 = slots(ROW3)
            q2 = joined(2, slots(ROW2), summed(SUM3))
            q1 = joined(1, slots(ROW1), summed(SUM2) + weighted(1, q3))
            q0 = joined(0, slots(ROW0), summed(SUM1) + weighted(0, q2))
            for level, q in enumerate((q0, q1, q2, q3)):
                if last:
                    for k in (0, 2):
                        for half in (0, 4):
                            rows = jnp.concatenate([q[k][half : half + 4], q[k + 1][half : half + 4]], axis=0)
                            top = 4 * half + 4 * k
                            qsend[level, top : top + 8, pl.ds(span, 128)] = rows
                else:
                    for k in range(4):
                        qbuf[level, 8 * k : 8 * k + 8, pl.ds(span, 128)] = q[k]
                total = total + ((q[0] * q[0] + q[1] * q[1]) + (q[2] * q[2] + q[3] * q[3]))
            return total

        return step

    def exchange(src, ring, count, send_sem, recv_sem, peer):
        def copy(j):
            return pltpu.make_async_remote_copy(
                src_ref=src,
                dst_ref=ring.at[j],
                send_sem=send_sem.at[j],
                recv_sem=recv_sem.at[j],
                device_id=peer(j),
                device_id_type=MESH,
            )

        copies = [copy(j) for j in sorted(range(1, count), key=lambda j: -min(j, count - j))]
        for item in copies:
            item.start()

        def finish():
            for item in reversed(copies):
                item.wait()

        return finish

    def reduce_start(total, ring_a, recv_a):
        part_a[...] = total
        ring_a[0] = total
        return exchange(part_a, ring_a, PEERS_A, ar_send_a, recv_a, peer_a)

    def reduce_second(finish, ring_a, ring_b, recv_b, ready=None):
        finish()
        if ready is not None:
            ready()
        total = jnp.sum(ring_a[...], axis=0)
        part_b[...] = total
        ring_b[0] = total
        return exchange(part_b, ring_b, CHIPS, ar_send_b, recv_b, peer_b)

    def reduce_rate(finish, ring_b):
        finish()
        total = jnp.sum(jnp.sum(ring_b[...], axis=0), axis=1, keepdims=True)
        return jnp.broadcast_to(STEP_SCALE / jnp.sqrt(total / ENTRIES + EPS), (8, 128))

    sends[0].wait()
    gather(1, [(0, diffs.at[1]), (-1, win1)])
    columns(None, (1,))
    next_round(1)
    payoffs(ROW0, ROW1)
    heard(2, along_node, known_node)
    announce(3, along_node, known_node)
    for copy in sends[1:4]:
        copy.wait()
    gather(0, [(0, diffs.at[0]), (-1, win0a), (-2, win0b)])
    gather(2, [(0, diffs.at[2]), (1, win2)])
    columns(None, (2,))
    sends[4].wait()
    sends[5].wait()
    gather(3, [(0, diffs.at[3]), (1, win3a), (2, win3b)])
    columns(None, (3,))
    total = payoffs(ROW1, ROWS, values_up(False))
    heard(2, along_board, known_board)
    first = reduce_start(total, ring_a1, ar_recv_a1)
    ready = functools.partial(heard, 3, along_node, known_node)
    rate = reduce_rate(reduce_second(first, ring_a1, ring_b1, ar_recv_b1, ready), ring_b1)
    columns(rate, (1, 2, 3))
    total = payoffs(SUM1, ROWS, values_up(True))
    first = reduce_start(total, ring_a2, ar_recv_a2)

    def back(idx, src, dst, step):
        return pltpu.make_async_remote_copy(
            src_ref=src,
            dst_ref=dst,
            send_sem=ret_send.at[idx],
            recv_sem=ret_recv.at[idx],
            device_id=at_node(step),
            device_id_type=MESH,
        )

    backs = [
        back(0, qsend.at[3], ret3a, 1),
        back(1, qsend.at[3, pl.ds(0, 16)], ret3b, 2),
        back(2, qsend.at[2, pl.ds(0, 16)], ret2, 1),
        back(3, qsend.at[0], ret0a, -1),
        back(4, qsend.at[0, pl.ds(16, 16)], ret0b, -2),
        back(5, qsend.at[1, pl.ds(16, 16)], ret1, -1),
    ]
    for copy in backs:
        copy.start()
    second = reduce_second(first, ring_a2, ring_b2, ar_recv_b2)

    def scatter(level, windows):
        rows = jnp.concatenate([ref[...] for _, _, ref in windows], axis=0)
        pick = []
        for step, half, ref in windows:
            shape = (SLOT_DEV, ref.shape[0])
            out_row = iota(shape, 0)
            col = iota(shape, 1) + 16 * half
            chain = 4 * jnp.right_shift(col, 4) + jnp.bitwise_and(col, 3)
            same_slot = jnp.bitwise_and(jnp.right_shift(col, 2), 3) == jnp.bitwise_and(out_row, 3)
            spot = places(chain)[level] + GROUPS * step
            hit = jnp.logical_and(same_slot, spot == jnp.right_shift(out_row, 2))
            pick.append(jnp.where(hit, 1.0, 0.0))
        out_values[0, level] = pick_rows(jnp.concatenate(pick, axis=1), rows)[:, 0:HANDS]

    backs[5].wait()
    scatter(1, [(0, 0, qsend.at[1]), (1, 1, ret1)])
    backs[3].wait()
    backs[4].wait()
    scatter(0, [(0, 0, qsend.at[0]), (1, 0, ret0a), (2, 1, ret0b)])
    backs[2].wait()
    scatter(2, [(0, 0, qsend.at[2]), (-1, 0, ret2)])
    backs[0].wait()
    backs[1].wait()
    scatter(3, [(0, 0, qsend.at[3]), (-1, 0, ret3a), (-2, 0, ret3b)])
    rate = reduce_rate(second, ring_b2)
    for level in range(LEVELS):
        out_logits[0, level] = own[level] + rate[0:1, 0:1] * out_values[0, level]


def write_out(logits_v, values_v, out_logits, out_values, sem):
    copies = [
        pltpu.make_async_copy(logits_v, out_logits, sem.at[0]),
        pltpu.make_async_copy(values_v, out_values, sem.at[1]),
    ]
    for copy in copies:
        copy.start()
    for copy in copies:
        copy.wait()


def per_device(
    logits, pot_size, node_type, parent_slot, range_one, range_two, hand_rank, live_mask
):
    small = (LEVELS, SLOT_DEV)
    rows = (SLOT_DEV, HANDS)
    wide = (SLOT_DEV, PAD)
    vmem = pltpu.VMEM
    dma = pltpu.SemaphoreType.DMA
    scratch = [
        vmem((LEVELS,) + rows, F32),
        vmem(small, F32),
        vmem(small, jnp.int32),
        pltpu.SMEM(small, jnp.int32),
        vmem((1, HANDS), F32),
        vmem((1, HANDS), F32),
        vmem((1, HANDS), jnp.int32),
        vmem((1, HANDS), jnp.int32),
        vmem((64, PAD), F32),
        vmem((PAD, 64), BF16),
        vmem((LEVELS, 24, PAD), F32),
        vmem((24, PAD), F32),
        vmem((8, PAD), F32),
        vmem((16, PAD), F32),
        vmem((16, PAD), F32),
        vmem((24, PAD), F32),
        vmem((16, PAD), F32),
        vmem((4,) + small, F32),
        vmem((4,) + small, jnp.int32),
        vmem((1, PAD), F32),
        vmem((1, PAD), F32),
        vmem((1, PAD), F32),
        vmem((1, PAD), F32),
        vmem((64, PAD), BF16),
        vmem((3, LEVELS, 4, 8, 128), F32),
        vmem((LEVELS, 24, PAD), F32),
        vmem((2,) + wide, F32),
        vmem((LEVELS,) + wide, F32),
        vmem((LEVELS,) + wide, F32),
        vmem((ROWS, DEEP), BF16),
        vmem((ROWS, PAD), BF16),
        vmem((DEEP, PAD), BF16),
        vmem((ROWS, PAD), F32),
        vmem((1, 128), F32),
        vmem((1, 128), F32),
        vmem((PEERS_A, 1, 128), F32),
        vmem((CHIPS, 1, 128), F32),
        vmem((PEERS_A, 1, 128), F32),
        vmem((CHIPS, 1, 128), F32),
        vmem(wide, F32),
        vmem((16, PAD), F32),
        vmem((16, PAD), F32),
        vmem((16, PAD), F32),
        vmem(wide, F32),
        vmem((16, PAD), F32),
        vmem((2, 8, PAD), F32),
        pltpu.SemaphoreType.REGULAR((4,)),
        pltpu.SemaphoreType.REGULAR((3,)),
        dma((10,)),
        dma((14,)),
        dma((14,)),
        dma((6,)),
        dma((6,)),
        dma((PEERS_A,)),
        dma((CHIPS,)),
        dma((PEERS_A,)),
        dma((CHIPS,)),
        dma((PEERS_A,)),
        dma((CHIPS,)),
    ]
    whole = jax.ShapeDtypeStruct(logits.shape, F32)
    free = pl.BlockSpec(memory_space=pl.ANY)
    table = card_rows()
    turned = table.T.copy()
    turned[:, CARDS] = 1.0
    found = pl.pallas_call(
        kernel,
        name="extragradient",
        out_shape=(whole, whole),
        in_specs=[free] * 10,
        out_specs=(pl.BlockSpec(memory_space=pltpu.VMEM),) * 2,
        scratch_shapes=scratch,
        compiler_params=pltpu.CompilerParams(
            collective_id=0, has_side_effects=True, vmem_limit_bytes=40 * 1024 * 1024
        ),
    )(
        *[
            pltpu.with_memory_space_constraint(value, pltpu.HBM)
            for value in (
                logits,
                pot_size,
                node_type,
                parent_slot,
                range_one,
                range_two,
                hand_rank,
                live_mask,
                jnp.asarray(table),
                jnp.asarray(turned, BF16),
            )
        ]
    )
    return pl.pallas_call(
        write_out,
        name="write_out",
        out_shape=(whole, whole),
        in_specs=[free] * 2,
        out_specs=(pl.BlockSpec(memory_space=pltpu.HBM),) * 2,
        scratch_shapes=[dma((2,))],
    )(*[pltpu.with_memory_space_constraint(value, pltpu.VMEM) for value in found])


def solution(mesh):
    placed = (
        P("board", None, "node", None),
        P(None, "node"),
        P(None, "node"),
        P(None, "node"),
        P("board", None),
        P("board", None),
        P("board", None),
        P("board", None),
    )
    return jax.shard_map(
        per_device,
        mesh=mesh,
        in_specs=placed,
        out_specs=(P("board", None, "node", None), P("board", None, "node", None)),
        check_vma=False,
    )
```
